32 devices in a mesh: ctx: 8 (over z, y), fsdp: 4 (over x, core).
Axes of the slice: x: 2, y: 2, z: 4, core: 2. Of those that a mesh axis runs over, the one named last changes fastest.
Arguments:
- inputs: bfloat16 [4, 4096, 768], P('fsdp', 'ctx'), may hold values from -6 to 6
- encoded: bfloat16 [4, 512, 768], P('fsdp', 'ctx'), may hold values from -6 to 6
- doc_lengths: int32 [4, 4], P('fsdp'), may hold values from 1 to 3840, 4096 in all within a row
- self_gain: bfloat16 [768], P('fsdp'), may hold values from 0.5 to 1.5
- self_query: bfloat16 [768, 768], P('fsdp'), may hold values from -0.0390625 to 0.0390625
- self_key: bfloat16 [768, 768], P('fsdp'), may hold values from -0.21875 to 0.21875
- self_value: bfloat16 [768, 768], P('fsdp'), may hold values from -0.21875 to 0.21875
- self_output: bfloat16 [768, 768], P('fsdp'), may hold values from -1.25 to 1.25
- bias_table: bfloat16 [32, 12], P('fsdp'), may hold values from -4 to 4
- cross_gain: bfloat16 [768], P('fsdp'), may hold values from 0.5 to 1.5
- cross_query: bfloat16 [768, 768], P('fsdp'), may hold values from -0.0390625 to 0.0390625
- cross_key: bfloat16 [768, 768], P('fsdp'), may hold values from -0.21875 to 0.21875
- cross_value: bfloat16 [768, 768], P('fsdp'), may hold values from -0.21875 to 0.21875
- cross_output: bfloat16 [768, 768], P('fsdp'), may hold values from -1.75 to 1.75
- ffn_gain: bfloat16 [768], P('fsdp'), may hold values from 0.5 to 1.5
- ffn_gate: bfloat16 [768, 2048], P(None, 'fsdp'), may hold values from -0.21875 to 0.21875
- ffn_up: bfloat16 [768, 2048], P(None, 'fsdp'), may hold values from -0.21875 to 0.21875
- ffn_down: bfloat16 [2048, 768], P('fsdp'), may hold values from -0.125 to 0.125
- cotangent: bfloat16 [4, 4096, 768], P('fsdp', 'ctx'), may hold values from -6 to 6
Outputs:
- outputs: bfloat16 [4, 4096, 768], P('fsdp', 'ctx')
- grad_inputs: bfloat16 [4, 4096, 768], P('fsdp', 'ctx')
- grad_encoded: bfloat16 [4, 512, 768], P('fsdp', 'ctx')
- grad_self_gain: float32 [768], P('fsdp')
- grad_self_query: float32 [768, 768], P('fsdp')
- grad_self_key: float32 [768, 768], P('fsdp')
- grad_self_value: float32 [768, 768], P('fsdp')
- grad_self_output: float32 [768, 768], P('fsdp')
- grad_bias_table: float32 [32, 12], P('fsdp')
- grad_cross_gain: float32 [768], P('fsdp')
- grad_cross_query: float32 [768, 768], P('fsdp')
- grad_cross_key: float32 [768, 768], P('fsdp')
- grad_cross_value: float32 [768, 768], P('fsdp')
- grad_cross_output: float32 [768, 768], P('fsdp')
- grad_ffn_gain: float32 [768], P('fsdp')
- grad_ffn_gate: float32 [768, 2048], P(None, 'fsdp')
- grad_ffn_up: float32 [768, 2048], P(None, 'fsdp')
- grad_ffn_down: float32 [2048, 768], P('fsdp')
The draws below stay inside these ranges and needn't reach their ends.
Inputs may be any that keep to these rules, and one draw needn't show every extreme that they name: `doc_lengths`: each row holds the lengths of the 4 documents packed in order into one sequence; they sum to 4096, and the longest is exactly 3840.
All inputs are finite; a program needn't handle non-finite values.
Results may differ from the reference program's by a relative error of at most 0.04.
Values may be sent and summed in bfloat16 or wider, within the bound.
No kernel may reach another device: no remote copies, remote signals or barrier semaphores. Data moves between devices by JAX's collectives and lax.ppermute only.
A program may use at most 320 MiB of HBM per device.

```python
import math
import jax
import jax.numpy as jnp
import numpy as np
from jax import lax

D = 768
H = 12
DH = 64
FF = 2048
NB = 32
MAXD = 128
DOCS = 4
TOK_DEV = 512
SEQS = 4
SEQ_LEN = 4096
ENC_LEN = 512


def block_scale(stream_key, dims, pieces, least, top_value):
    loudness = 1.0
    for dim, parts in pieces:
        heights = jax.random.uniform(jax.random.fold_in(jax.random.fold_in(stream_key, 6), dim), (parts,), jnp.float32, least / len(pieces), top_value / len(pieces))
        loudness = loudness * jnp.repeat(jnp.exp(heights), dims[dim] // parts).reshape((-1,) + (1,) * (len(dims) - 1 - dim))
    return loudness


def profile(count, total, limit, skew):
    weights = [(1 << 20) // math.isqrt(standing ** skew) + 1 for standing in range(2, count + 1)]
    spare, given = total - limit - (count - 1), [1] * (count - 1)
    while spare > 0:
        candidates = [i for i in range(count - 1) if given[i] < limit]
        whole, budget = sum([weights[i] for i in candidates]), spare
        for i in candidates:
            addition = min(limit - given[i], max(1, budget * weights[i] // whole), spare)
            given[i] = given[i] + addition
            spare = spare - addition
    return np.array([limit] + given)


def ragged_sizes(own_key, count, total, reach, lean):
    if count == 2:
        one = jax.random.randint(own_key, (), max(1, total - reach), min(reach, total - 1) + 1)
        return jnp.stack([one, total - one])
    tallies = jnp.asarray(profile(count, total, reach, lean), jnp.int32)
    pairs = (count - 1) // 2
    donor, receiver = tallies[1:1 + 2 * pairs:2], tallies[2:2 + 2 * pairs:2]
    slack = jnp.minimum(donor - 1, reach - receiver)
    moved = jax.random.randint(jax.random.fold_in(own_key, 1), (pairs,), 0, 1 << 20) % (slack + 1)
    tallies = tallies.at[1:1 + 2 * pairs:2].set(donor - moved).at[2:2 + 2 * pairs:2].set(receiver + moved)
    return tallies[jax.random.permutation(jax.random.fold_in(own_key, 2), count)]


def gaussian(own_key, extent, spread, reach, pieces=(), kind=jnp.bfloat16):
    loudness = block_scale(own_key, extent, pieces, -0.22, 0.18) if pieces else 1.0
    values = jax.random.normal(own_key, extent, jnp.float32) * spread * loudness
    return jnp.minimum(jnp.maximum(values, -reach), reach).astype(kind)


def setup_inputs(seed: int = 0) -> dict:
    key_list = jax.random.split(jax.random.key(seed), 20)
    return {
        "inputs": gaussian(key_list[0], (SEQS, SEQ_LEN, D), 1.0, 6.0, ((0, 4), (1, 8))),
        "encoded": gaussian(key_list[1], (SEQS, ENC_LEN, D), 1.0, 6.0, ((0, 4), (1, 8))),
        "doc_lengths": jax.vmap(lambda own: ragged_sizes(own, DOCS, SEQ_LEN, SEQ_LEN - TOK_DEV // 2, 0))(jax.random.split(key_list[2], SEQS)).reshape((SEQS, DOCS)).astype(jnp.int32),
        "self_gain": jnp.clip(1.0 + 0.1 * jax.random.normal(key_list[3], (D,), jnp.float32), 0.5, 1.5).astype(jnp.bfloat16),
        "self_query": gaussian(key_list[4], (D, D), (32 * D) ** -0.5, 0.0390625, ((0, 4),)),
        "self_key": gaussian(key_list[5], (D, D), D ** -0.5, 0.21875, ((0, 4),)),
        "self_value": gaussian(key_list[6], (D, D), D ** -0.5, 0.21875, ((0, 4),)),
        "self_output": gaussian(key_list[7], (D, D), (max(D // 32, 8)) ** -0.5, 1.25, ((0, 4),)),
        "bias_table": gaussian(key_list[8], (NB, H), 1.0, 4.0, ((0, 4),)),
        "cross_gain": jnp.clip(1.0 + 0.1 * jax.random.normal(key_list[9], (D,), jnp.float32), 0.5, 1.5).astype(jnp.bfloat16),
        "cross_query": gaussian(key_list[10], (D, D), (32 * D) ** -0.5, 0.0390625, ((0, 4),)),
        "cross_key": gaussian(key_list[11], (D, D), D ** -0.5, 0.21875, ((0, 4),)),
        "cross_value": gaussian(key_list[12], (D, D), D ** -0.5, 0.21875, ((0, 4),)),
        "cross_output": gaussian(key_list[13], (D, D), (max(D // 64, 8)) ** -0.5, 1.75, ((0, 4),)),
        "ffn_gain": jnp.clip(1.0 + 0.1 * jax.random.normal(key_list[14], (D,), jnp.float32), 0.5, 1.5).astype(jnp.bfloat16),
        "ffn_gate": gaussian(key_list[15], (D, FF), D ** -0.5, 0.21875, ((1, 4),)),
        "ffn_up": gaussian(key_list[16], (D, FF), D ** -0.5, 0.21875, ((1, 4),)),
        "ffn_down": gaussian(key_list[17], (FF, D), FF ** -0.5, 0.125, ((0, 4),)),
        "cotangent": gaussian(key_list[18], (SEQS, SEQ_LEN, D), 1.0, 6.0, ((0, 4), (1, 8))),
    }


@jax.custom_vjp
def low(v):
    return lax.optimization_barrier(v.astype(jnp.bfloat16)).astype(jnp.float32)

@jax.custom_vjp
def low_back(v):
    return v

def low_keep(v):
    return (low(v), None)

def low_pass(kept, grad):
    return (grad,)

def back_keep(v):
    return (v, None)

def back_low(kept, grad):
    return (low(grad),)
low.defvjp(low_keep, low_pass)
low_back.defvjp(back_keep, back_low)
epsilon = 1e-06
highest = lax.Precision.HIGHEST
negative = -1e+30

def rounded(vector):
    return low(low_back(vector))

def matmul(matrix_left, matrix_right):
    return jnp.dot(matrix_left, matrix_right, precision=highest, preferred_element_type=jnp.float32)

def rms_norm(vector, scaling):
    factor = lax.rsqrt(lax.optimization_barrier(jnp.mean(vector * vector, axis=-1, keepdims=True)) + epsilon)
    return vector * factor * scaling

def bucket_of(offset):
    exact_span = NB // 2
    bucket = jnp.minimum(offset, exact_span)
    for section_index in range(1, exact_span):
        threshold = math.ceil(exact_span * (MAXD / exact_span) ** (section_index / exact_span))
        bucket = bucket + (offset >= threshold).astype(jnp.int32)
    return bucket.astype(jnp.int32)

def document_of(positions, doc_ends):
    return lax.optimization_barrier(jnp.sum((positions[:, None] >= doc_ends[None, :-1]).astype(jnp.int32), axis=1)).astype(jnp.int32)

def self_attention(queries, key_proj, value_proj, bias_rows, doc_ends):
    length = key_proj.shape[0]
    block_rows = min(512, length)
    key_heads = key_proj.reshape(length, H, DH)
    value_heads = value_proj.reshape(length, H, DH)
    key_pos = jnp.arange(length, dtype=jnp.int32)
    key_doc = document_of(key_pos, doc_ends)

    def one_block(block_input):
        query_block, first_row = block_input
        query_pos = first_row + jnp.arange(block_rows, dtype=jnp.int32)
        scores = jnp.einsum('qhd,khd->hqk', query_block.reshape(block_rows, H, DH), key_heads, precision=highest)
        offset = jnp.maximum(query_pos[:, None] - key_pos[None, :], 0)
        scores = low_back(scores + jnp.transpose(bias_rows[bucket_of(offset)], (2, 0, 1)))
        allowed = (key_pos[None, :] <= query_pos[:, None]) & (document_of(query_pos, doc_ends)[:, None] == key_doc[None, :])
        scores = jnp.where(allowed[None], scores, negative)
        weights_low = low(jax.nn.softmax(scores, axis=-1))
        weighted = jnp.einsum('hqk,khd->qhd', weights_low, value_heads, precision=highest)
        return weighted.reshape(block_rows, D)
    starts = jnp.arange(length // block_rows, dtype=jnp.int32) * block_rows
    result = lax.map(jax.checkpoint(one_block), (queries.reshape(length // block_rows, block_rows, D), starts))
    return result.reshape(length, D)

def cross_attention(queries, key_proj, value_proj):
    length = queries.shape[0]
    block_rows = min(512, length)
    key_heads = key_proj.reshape(key_proj.shape[0], H, DH)
    value_heads = value_proj.reshape(value_proj.shape[0], H, DH)

    def one_block(query_block):
        scores = low_back(jnp.einsum('qhd,khd->hqk', query_block.reshape(block_rows, H, DH), key_heads, precision=highest))
        weights_low = low(jax.nn.softmax(scores, axis=-1))
        weighted = jnp.einsum('hqk,khd->qhd', weights_low, value_heads, precision=highest)
        return weighted.reshape(block_rows, D)
    result = lax.map(jax.checkpoint(one_block), queries.reshape(length // block_rows, block_rows, D))
    return result.reshape(length, D)

def layer(params, states, encoder, doc_ends):
    gain_self, w_query, w_key, w_value, w_output, bias_rows, gain_cross, c_query, c_key, c_value, c_output, gain_ffn, w_gate, w_up, w_down = params
    normed_one = low(rms_norm(states, gain_self))
    query_proj = rounded(matmul(normed_one, w_query))
    key_proj = rounded(matmul(normed_one, w_key))
    value_proj = rounded(matmul(normed_one, w_value))
    attended = rounded(self_attention(query_proj, key_proj, value_proj, bias_rows, doc_ends))
    first_sum = states + low_back(matmul(attended, w_output))
    normed_two = low(rms_norm(first_sum, gain_cross))
    cross_queries = rounded(matmul(normed_two, c_query))
    cross_keys = rounded(matmul(encoder, c_key))
    cross_values = rounded(matmul(encoder, c_value))
    cross_out = rounded(cross_attention(cross_queries, cross_keys, cross_values))
    second_sum = first_sum + low_back(matmul(cross_out, c_output))
    normed_three = low(rms_norm(second_sum, gain_ffn))
    gate_proj = low_back(matmul(normed_three, w_gate))
    up_proj = low_back(matmul(normed_three, w_up))
    hidden = low(jax.nn.gelu(gate_proj, approximate=True) * up_proj)
    return second_sum + matmul(hidden, w_down)

def reference(inputs, encoded, doc_lengths, self_gain, self_query, self_key, self_value, self_output, bias_table, cross_gain, cross_query, cross_key, cross_value, cross_output, ffn_gain, ffn_gate, ffn_up, ffn_down, cotangent):
    params = tuple((weight.astype(jnp.float32) for weight in (self_gain, self_query, self_key, self_value, self_output, bias_table, cross_gain, cross_query, cross_key, cross_value, cross_output, ffn_gain, ffn_gate, ffn_up, ffn_down)))

    def one_sequence(totals, element):
        states, encoder, lengths, outer_grad = element
        doc_ends = jnp.cumsum(lengths).astype(jnp.int32)

        def forward(weights, states_in, encoder_in):
            return layer(weights, states_in, encoder_in, doc_ends)
        output, pull_back = jax.vjp(forward, params, states.astype(jnp.float32), encoder.astype(jnp.float32))
        grad_params, grad_states, grad_encoder = pull_back(outer_grad.astype(jnp.float32))
        totals = tuple((total + grad_one for total, grad_one in zip(totals, grad_params)))
        return (totals, (output.astype(jnp.bfloat16), grad_states.astype(jnp.bfloat16), grad_encoder.astype(jnp.bfloat16)))
    zero_grads = tuple((jnp.zeros(weight.shape, jnp.float32) for weight in params))
    totals, (outputs, grad_inputs, grad_encoded) = lax.scan(one_sequence, zero_grads, (inputs, encoded, doc_lengths, cotangent))
    return (outputs, grad_inputs, grad_encoded, totals[0], totals[1], totals[2], totals[3], totals[4], totals[5], totals[6], totals[7], totals[8], totals[9], totals[10], totals[11], totals[12], totals[13], totals[14])
```

```python
import functools
import math

import jax
import jax.numpy as jnp
from jax import lax
from jax.experimental import pallas as pl
from jax.experimental.pallas import tpu as pltpu
from jax.sharding import PartitionSpec as P

D = 768
H = 12
DH = 64
NB = 32
MAXD = 128
GROUPS = 4
GH = H // GROUPS
GL = GH * DH
GP = 256

epsilon = 1e-06
negative = -1e30
f32 = jnp.float32
bf16 = jnp.bfloat16
VMEM_LIMIT = 60 * 1024 * 1024


def thresholds():
    exact = NB // 2
    return list(range(1, exact + 1)) + [
        math.ceil(exact * (MAXD / exact) ** (t / exact)) for t in range(1, exact)
    ]


def matmul(a, b):
    return jnp.dot(a, b, preferred_element_type=f32)


def left_matmul(a, b):
    return lax.dot_general(a, b, (((0,), (0,)), ((), ())), preferred_element_type=f32)


def right_matmul(a, b):
    return lax.dot_general(a, b, (((1,), (1,)), ((), ())), preferred_element_type=f32)


def inverse_rms(v):
    return lax.rsqrt(jnp.mean(v * v, axis=-1, keepdims=True) + epsilon)


def norm_back(v, g, e):
    r = inverse_rms(v)
    ge = e * g
    grad_v = r * ge - v * (r * r * r * jnp.mean(ge * v, axis=-1, keepdims=True))
    return grad_v, jnp.sum(e * v * r, axis=0)


def flip(x):
    return x.astype(f32).T.astype(bf16)


def sub_of(i, split, parts):
    return jnp.where(i % 2 == 0, split, parts - 1 - split)


def doc_start(pos, meta):
    start = jnp.zeros_like(pos)
    for d in range(3):
        start = jnp.where(pos >= meta[d], meta[d], start)
    return start


def tile_bias(table, h, base, rows, cols):
    offset = base + (
        lax.broadcasted_iota(jnp.int32, (rows, cols), 1)
        - lax.broadcasted_iota(jnp.int32, (rows, cols), 0)
    )
    bias = jnp.full((rows, cols), table[0, h], f32)
    for b, at in enumerate(thresholds()):
        bias = jnp.where(offset >= at, table[b + 1, h], bias)
    return bias


def head_rows(x_t, h):
    parts = []
    if h:
        parts.append(jnp.zeros((h * DH, x_t.shape[1]), x_t.dtype))
    parts.append(x_t[h * DH : (h + 1) * DH])
    parts.append(jnp.zeros((GP - (h + 1) * DH, x_t.shape[1]), x_t.dtype))
    return jnp.concatenate(parts, axis=0)


def head_lanes(x, h):
    lane = lax.broadcasted_iota(jnp.int32, x.shape, 1)
    keep = (lane >= h * DH) & (lane < (h + 1) * DH)
    return jnp.where(keep, x.astype(f32), 0.0).astype(bf16)


def sweep(meta, first, block, step):
    start_lo = doc_start(first, meta)
    start_hi = doc_start(first + block - 1, meta)
    far_end = jnp.maximum(first // block - 1, 0)
    lo = jnp.minimum(start_lo // block, far_end)
    mid = jnp.clip((start_hi + block - 1) // block, lo, far_end)

    def masked(t, carry):
        step(pl.multiple_of(t * block, block), block, "masked")
        return carry

    lax.fori_loop(lo, mid, masked, 0)
    odd = (far_end - mid) % 2

    @pl.when(odd == 1)
    def _():
        step(pl.multiple_of(mid * block, block), block, "far")

    def far(t, carry):
        step(pl.multiple_of((mid + odd + 2 * t) * block, block), 2 * block, "far")
        return carry

    lax.fori_loop(0, (far_end - mid) // 2, far, 0)

    @pl.when(first > 0)
    def _():
        step(pl.multiple_of(jnp.maximum(first - block, 0), block), block, "prev")

    step(pl.multiple_of(first, block), block, "diag")


def tile_mask(kind, k0, rows, first, block, starts):
    key = k0 + lax.broadcasted_iota(jnp.int32, (rows, block), 0)
    mask = key >= starts
    if kind == "diag":
        query = first + lax.broadcasted_iota(jnp.int32, (rows, block), 1)
        mask = mask & (key <= query)
    return mask


def self_forward_kernel(
    parts, tok, meta, table, q_ref, k_ref, v_ref, o_ref, full_ref, lse_ref,
    v_t, bias, acc, top, total, q_masked,
):
    i = pl.program_id(0)
    block = tok // parts
    first = i * tok + sub_of(i, meta[3], parts) * block

    @pl.when(i == 0)
    def _():
        for h in range(GH):
            bias[h, 0] = tile_bias(table, h, 0, block, block)
            bias[h, 1] = tile_bias(table, h, block, block, block)

        def turn(t, carry):
            at = pl.multiple_of(t * block, block)
            v_t[:, pl.ds(at, block)] = flip(v_ref[pl.ds(at, block), :])
            return carry

        lax.fori_loop(0, v_ref.shape[0] // block, turn, 0)

    q_t = flip(q_ref[...])
    for h in range(GH):
        q_masked[h] = head_rows(q_t, h)
    top[...] = jnp.full_like(top, negative)
    total[...] = jnp.zeros_like(total)
    acc[...] = jnp.zeros_like(acc)
    starts = doc_start(first + lax.broadcasted_iota(jnp.int32, (1, block), 1), meta)

    def step(k0, rows, kind):
        k_tile = k_ref[pl.ds(k0, rows), :]
        if kind != "far":
            mask = tile_mask(kind, k0, rows, first, block, starts)
        for h in range(GH):
            s = matmul(k_tile, q_masked[h])
            shift = table[NB - 1, h]
            if kind == "diag":
                s, shift = s + bias[h, 0], 0.0
            elif kind == "prev":
                s, shift = s + bias[h, 1], 0.0
            if kind != "far":
                s = jnp.where(mask, s, negative)
            old = top[h : h + 1]
            new = jnp.maximum(old, jnp.max(s, axis=0, keepdims=True) + shift)
            scale = jnp.exp(old - new)
            p = jnp.exp(s - (new - shift))
            top[h : h + 1] = new
            total[h : h + 1] = total[h : h + 1] * scale + jnp.sum(p, axis=0, keepdims=True)
            rows_h = slice(h * DH, (h + 1) * DH)
            acc[rows_h] = acc[rows_h] * scale + matmul(
                v_t[rows_h, pl.ds(k0, rows)], p.astype(bf16)
            )

    sweep(meta, first, block, step)
    for h in range(GH):
        rows_h = slice(h * DH, (h + 1) * DH)
        acc[rows_h] = acc[rows_h] / total[h : h + 1]
    full_ref[...] = acc[:GL]
    o_ref[0] = acc[...].T[:, :GL].astype(bf16)
    lse_ref[...] = jnp.zeros_like(lse_ref)
    lse_ref[0:GH] = top[0:GH] + jnp.log(total[0:GH])


def self_backward_kernel(
    parts, tok, meta, table, q_ref, k_ref, v_ref, do_ref, full_ref, lse_ref, out_ref, tab_ref,
    k_t, bias, dk, dv, dq_t, near, far_sum, q_masked, do_masked, q_lanes, do_lanes, delta,
):
    i = pl.program_id(0)
    block = tok // parts
    first = i * tok + sub_of(i, meta[3], parts) * block
    length = k_ref.shape[0]

    @pl.when(i == 0)
    def _():
        for h in range(GH):
            bias[h, 0] = tile_bias(table, h, 0, block, block)
            bias[h, 1] = tile_bias(table, h, block, block, block)
        near[...] = jnp.zeros_like(near)
        far_sum[...] = jnp.zeros_like(far_sum)

        def turn(t, carry):
            at = pl.multiple_of(t * block, block)
            rows = pl.ds(at, block)
            k_t[:, rows] = flip(k_ref[rows, :])
            dk[rows, :] = jnp.zeros((block, GP), f32)
            dv[rows, :] = jnp.zeros((block, GP), f32)
            out_ref[rows, 0:GP] = jnp.zeros((block, GP), bf16)
            return carry

        lax.fori_loop(0, length // block, turn, 0)

    do_full = do_ref[0]
    q_t = flip(q_ref[...])
    do_t = do_full.astype(f32).T
    for h in range(GH):
        rows_h = slice(h * DH, (h + 1) * DH)
        delta[h : h + 1] = jnp.sum(do_t[rows_h] * full_ref[rows_h], axis=0, keepdims=True)
        q_masked[h] = head_rows(q_t, h)
        do_masked[h] = head_rows(do_t.astype(bf16), h)
        q_lanes[h * block : (h + 1) * block] = head_lanes(q_ref[...], h)
        do_lanes[h * block : (h + 1) * block] = head_lanes(do_full, h)
    dq_t[...] = jnp.zeros_like(dq_t)
    starts = doc_start(first + lax.broadcasted_iota(jnp.int32, (1, block), 1), meta)

    def step(k0, rows, kind):
        at = pl.ds(k0, rows)
        k_tile = k_ref[at, :]
        v_tile = v_ref[at, :]
        if kind != "far":
            mask = tile_mask(kind, k0, rows, first, block, starts)
        probs, grads = [], []
        for h in range(GH):
            s = matmul(k_tile, q_masked[h])
            shift = lse_ref[h : h + 1]
            if kind == "diag":
                s = s + bias[h, 0]
            elif kind == "prev":
                s = s + bias[h, 1]
            else:
                shift = shift - table[NB - 1, h]
            p = jnp.exp(s - shift)
            if kind != "far":
                p = jnp.where(mask, p, 0.0)
            ds = p * (matmul(v_tile, do_masked[h]) - delta[h : h + 1])
            if kind == "diag":
                near[h, 0] += ds
            elif kind == "prev":
                near[h, 1] += ds
            else:
                far_sum[h : h + 1] += jnp.sum(ds, axis=0, keepdims=True)
            probs.append(p.astype(bf16))
            grads.append(ds.astype(bf16))
            rows_h = slice(h * DH, (h + 1) * DH)
            dq_t[rows_h] += matmul(k_t[rows_h, at], grads[h])
        dv[at, :] += matmul(jnp.concatenate(probs, axis=1), do_lanes[...])
        dk[at, :] += matmul(jnp.concatenate(grads, axis=1), q_lanes[...])

    sweep(meta, first, block, step)
    out_ref[pl.ds(pl.multiple_of(first, block), block), 0:GP] = dq_t[...].T.astype(bf16)

    @pl.when(i == pl.num_programs(0) - 1)
    def _():
        def emit(t, carry):
            rows = pl.ds(pl.multiple_of(t * block, block), block)
            out_ref[rows, GP : 2 * GP] = dk[rows, :].astype(bf16)
            out_ref[rows, 2 * GP : 3 * GP] = dv[rows, :].astype(bf16)
            return carry

        lax.fori_loop(0, length // block, emit, 0)
        offset = lax.broadcasted_iota(jnp.int32, (block, block), 1) - lax.broadcasted_iota(
            jnp.int32, (block, block), 0
        )
        edges = [None] + thresholds()
        for h in range(GH):
            tails = []
            for at in edges:
                if at is None:
                    part = near[h, 0] + near[h, 1]
                else:
                    part = jnp.where(offset >= at, near[h, 0], 0.0) + jnp.where(
                        offset + block >= at, near[h, 1], 0.0
                    )
                tails.append(jnp.sum(part, axis=0, keepdims=True))
            for b in range(NB):
                if b + 1 < NB:
                    row = tails[b] - tails[b + 1]
                else:
                    row = tails[b] + far_sum[h : h + 1]
                tab_ref[h * NB + b : h * NB + b + 1] = row


def self_specs(parts, tok, length):
    block = tok // parts
    q_spec = pl.BlockSpec((block, GP), lambda i, m: (i * parts + sub_of(i, m[3], parts), 0))
    k_spec = pl.BlockSpec((length, GP), lambda i, m: (0, 1), pipeline_mode=pl.Buffered(1))
    v_spec = pl.BlockSpec((length, GP), lambda i, m: (0, 2), pipeline_mode=pl.Buffered(1))
    table_spec = pl.BlockSpec(memory_space=pltpu.SMEM)
    return table_spec, q_spec, k_spec, v_spec


def pair_count(length):
    return GH * length * length // 8


def self_forward(qkv, meta, table, parts, count, tok):
    length = qkv.shape[0]
    block = tok // parts
    rows = count * block
    return pl.pallas_call(
        functools.partial(self_forward_kernel, parts, tok),
        grid_spec=pltpu.PrefetchScalarGridSpec(
            num_scalar_prefetch=1,
            grid=(count,),
            in_specs=list(self_specs(parts, tok, length)),
            out_specs=[
                pl.BlockSpec((1, block, GL), lambda i, m: (i, 0, 0)),
                pl.BlockSpec((GL, block), lambda i, m: (0, i)),
                pl.BlockSpec((8, block), lambda i, m: (0, i)),
            ],
            scratch_shapes=[
                pltpu.VMEM((GP, length), bf16),
                pltpu.VMEM((GH, 2, block, block), f32),
                pltpu.VMEM((GP, block), f32),
                pltpu.VMEM((8, block), f32),
                pltpu.VMEM((8, block), f32),
                pltpu.VMEM((GH, GP, block), bf16),
            ],
        ),
        out_shape=[
            jax.ShapeDtypeStruct((count, block, GL), bf16),
            jax.ShapeDtypeStruct((GL, rows), f32),
            jax.ShapeDtypeStruct((8, rows), f32),
        ],
        compiler_params=pltpu.CompilerParams(vmem_limit_bytes=VMEM_LIMIT),
        cost_estimate=pl.CostEstimate(
            flops=pair_count(length) * 1024,
            transcendentals=pair_count(length),
            bytes_accessed=length * GP * 8,
        ),
        name="self_forward",
    )(meta, table, qkv, qkv, qkv)


def self_backward(qkv, meta, table, d_o, full, lse, parts, count, tok):
    length = qkv.shape[0]
    block = tok // parts
    return pl.pallas_call(
        functools.partial(self_backward_kernel, parts, tok),
        grid_spec=pltpu.PrefetchScalarGridSpec(
            num_scalar_prefetch=1,
            grid=(count,),
            in_specs=list(self_specs(parts, tok, length))
            + [
                pl.BlockSpec((1, block, GP), lambda i, m: (i, 0, 0)),
                pl.BlockSpec((GL, block), lambda i, m: (0, i)),
                pl.BlockSpec((8, block), lambda i, m: (0, i)),
            ],
            out_specs=[
                pl.BlockSpec((length, 3 * GP), lambda i, m: (0, 0), pipeline_mode=pl.Buffered(1)),
                pl.BlockSpec((GH * NB, block), lambda i, m: (0, 0)),
            ],
            scratch_shapes=[
                pltpu.VMEM((GP, length), bf16),
                pltpu.VMEM((GH, 2, block, block), f32),
                pltpu.VMEM((length, GP), f32),
                pltpu.VMEM((length, GP), f32),
                pltpu.VMEM((GP, block), f32),
                pltpu.VMEM((GH, 2, block, block), f32),
                pltpu.VMEM((8, block), f32),
                pltpu.VMEM((GH, GP, block), bf16),
                pltpu.VMEM((GH, GP, block), bf16),
                pltpu.VMEM((GH * block, GP), bf16),
                pltpu.VMEM((GH * block, GP), bf16),
                pltpu.VMEM((8, block), f32),
            ],
        ),
        out_shape=[
            jax.ShapeDtypeStruct((length, 3 * GP), bf16),
            jax.ShapeDtypeStruct((GH * NB, block), f32),
        ],
        compiler_params=pltpu.CompilerParams(vmem_limit_bytes=VMEM_LIMIT),
        cost_estimate=pl.CostEstimate(
            flops=pair_count(length) * 2560,
            transcendentals=pair_count(length),
            bytes_accessed=length * GP * 16,
        ),
        name="self_backward",
    )(meta, table, qkv, qkv, qkv, d_o, full, lse)


PAIR = 2 * DH


def pair_rows(x_t, h):
    zeros = jnp.zeros((DH, x_t.shape[1]), x_t.dtype)
    own = x_t[h * DH : (h + 1) * DH]
    return jnp.concatenate([own, zeros] if h == 0 else [zeros, own], axis=0)


def cross_forward_kernel(q_ref, k_ref, v_ref, o_ref, full_ref, lse_ref, v_t, q_t):
    tok = q_ref.shape[0]
    chunk = math.gcd(tok, 256)
    v_t[...] = flip(v_ref[...])
    q_t[...] = flip(q_ref[...])
    lse_ref[...] = jnp.zeros_like(lse_ref)
    for at in range(0, tok, chunk):
        cols = slice(at, at + chunk)
        for h in range(2):
            rows_h = slice(h * DH, (h + 1) * DH)
            s = matmul(k_ref[...], pair_rows(q_t[:, cols], h))
            top = jnp.max(s, axis=0, keepdims=True)
            p = jnp.exp(s - top)
            total = jnp.sum(p, axis=0, keepdims=True)
            full_ref[rows_h, cols] = matmul(v_t[rows_h], p.astype(bf16)) / total
            lse_ref[h : h + 1, cols] = top + jnp.log(total)
    o_ref[...] = full_ref[...].T.astype(bf16)


def cross_backward_kernel(
    q_ref, k_ref, v_ref, do_ref, full_ref, lse_ref, dq_ref, dk_ref, dv_ref, k_t, q_t, do_t, dq_t,
    dk, dv,
):
    tok = q_ref.shape[0]
    chunk = math.gcd(tok, 256)
    k_t[...] = flip(k_ref[...])
    q_t[...] = flip(q_ref[...])
    do_t[...] = do_ref[...].astype(f32).T
    for at in range(0, tok, chunk):
        cols = slice(at, at + chunk)
        probs, grads, q_lanes, do_lanes = [], [], [], []
        for h in range(2):
            rows_h = slice(h * DH, (h + 1) * DH)
            s = matmul(k_ref[...], pair_rows(q_t[:, cols], h))
            p = jnp.exp(s - lse_ref[h : h + 1, cols])
            delta = jnp.sum(do_t[rows_h, cols] * full_ref[rows_h, cols], axis=0, keepdims=True)
            dp = matmul(v_ref[...], pair_rows(do_t[:, cols].astype(bf16), h))
            ds = (p * (dp - delta)).astype(bf16)
            probs.append(p.astype(bf16))
            grads.append(ds)
            dq_t[rows_h, cols] = matmul(k_t[rows_h], ds)
            q_lanes.append(head_lanes(q_ref[cols, :], h))
            do_lanes.append(head_lanes(do_ref[cols, :], h))
        part_v = matmul(jnp.concatenate(probs, axis=1), jnp.concatenate(do_lanes, axis=0))
        part_k = matmul(jnp.concatenate(grads, axis=1), jnp.concatenate(q_lanes, axis=0))
        if at == 0:
            dv[...] = part_v
            dk[...] = part_k
        else:
            dv[...] += part_v
            dk[...] += part_k
    dq_ref[...] = dq_t[...].T.astype(bf16)
    dk_ref[...] = dk[...].astype(bf16)
    dv_ref[...] = dv[...].astype(bf16)


def cross_forward(q, k, v):
    tok, enc = q.shape[0], k.shape[0]
    pairs = H // 2
    col = lambda p: (0, p)
    row = lambda p: (p, 0)
    return pl.pallas_call(
        cross_forward_kernel,
        grid=(pairs,),
        in_specs=[
            pl.BlockSpec((tok, PAIR), col),
            pl.BlockSpec((enc, PAIR), col),
            pl.BlockSpec((enc, PAIR), col),
        ],
        out_specs=[
            pl.BlockSpec((tok, PAIR), col),
            pl.BlockSpec((PAIR, tok), row),
            pl.BlockSpec((8, tok), row),
        ],
        out_shape=[
            jax.ShapeDtypeStruct((tok, D), bf16),
            jax.ShapeDtypeStruct((D, tok), f32),
            jax.ShapeDtypeStruct((8 * pairs, tok), f32),
        ],
        scratch_shapes=[pltpu.VMEM((PAIR, enc), bf16), pltpu.VMEM((PAIR, tok), bf16)],
        compiler_params=pltpu.CompilerParams(vmem_limit_bytes=VMEM_LIMIT),
        cost_estimate=pl.CostEstimate(
            flops=H * tok * enc * 1024, transcendentals=H * tok * enc, bytes_accessed=D * tok * 12
        ),
        name="cross_forward",
    )(q, k, v)


def cross_backward(q, k, v, d_o, full, lse):
    tok, enc = q.shape[0], k.shape[0]
    pairs = H // 2
    col = lambda p: (0, p)
    row = lambda p: (p, 0)
    return pl.pallas_call(
        cross_backward_kernel,
        grid=(pairs,),
        in_specs=[
            pl.BlockSpec((tok, PAIR), col),
            pl.BlockSpec((enc, PAIR), col),
            pl.BlockSpec((enc, PAIR), col),
            pl.BlockSpec((tok, PAIR), col),
            pl.BlockSpec((PAIR, tok), row),
            pl.BlockSpec((8, tok), row),
        ],
        out_specs=[
            pl.BlockSpec((tok, PAIR), col),
            pl.BlockSpec((enc, PAIR), col),
            pl.BlockSpec((enc, PAIR), col),
        ],
        out_shape=[
            jax.ShapeDtypeStruct((tok, D), bf16),
            jax.ShapeDtypeStruct((enc, D), bf16),
            jax.ShapeDtypeStruct((enc, D), bf16),
        ],
        scratch_shapes=[
            pltpu.VMEM((PAIR, enc), bf16),
            pltpu.VMEM((PAIR, tok), bf16),
            pltpu.VMEM((PAIR, tok), f32),
            pltpu.VMEM((PAIR, tok), f32),
            pltpu.VMEM((enc, PAIR), f32),
            pltpu.VMEM((enc, PAIR), f32),
        ],
        compiler_params=pltpu.CompilerParams(vmem_limit_bytes=VMEM_LIMIT),
        cost_estimate=pl.CostEstimate(
            flops=H * tok * enc * 2560, transcendentals=H * tok * enc, bytes_accessed=D * tok * 20
        ),
        name="cross_backward",
    )(q, k, v, d_o, full, lse)


def gelu_pair(v):
    inner = math.sqrt(2 / math.pi) * (v + 0.044715 * (v * v * v))
    t = jnp.tanh(inner)
    half = 0.5 * (1.0 + t)
    slope = half + 0.5 * v * (1.0 - t * t) * (
        math.sqrt(2 / math.pi) * (1.0 + 3 * 0.044715 * (v * v))
    )
    return v * half, slope


def ffn_kernel(
    x_ref, c_ref, gate_ref, up_ref, down_ref, out_ref, gx_ref, dg_ref, du_ref, dd_ref, x_t
):
    f = pl.program_id(0)

    @pl.when(f == 0)
    def _():
        x_t[...] = flip(x_ref[...])
        out_ref[...] = jnp.zeros_like(out_ref)
        gx_ref[...] = jnp.zeros_like(gx_ref)

    x = x_ref[...]
    c = c_ref[...]
    w_gate, w_up, w_down = gate_ref[0], up_ref[0], down_ref[0]
    gate = matmul(x, w_gate)
    up = matmul(x, w_up)
    act, slope = gelu_pair(gate)
    hidden_full = act * up
    hidden = hidden_full.astype(bf16)
    out_ref[...] += matmul(hidden, w_down)
    grad_hidden = right_matmul(c, w_down)
    dd_ref[0] = matmul(hidden.astype(f32).T.astype(bf16), c).astype(bf16)
    grad_gate = (grad_hidden * up * slope).astype(bf16)
    grad_up = (grad_hidden * act).astype(bf16)
    dg_ref[0] = matmul(x_t[...], grad_gate).astype(bf16)
    du_ref[0] = matmul(x_t[...], grad_up).astype(bf16)
    gx_ref[...] += right_matmul(grad_gate, w_gate) + right_matmul(grad_up, w_up)


def ffn(x, c, gate, up, down):
    tok = x.shape[0]
    parts, _, width = gate.shape
    whole = pl.BlockSpec((tok, D), lambda f: (0, 0))
    wide = pl.BlockSpec((1, D, width), lambda f: (f, 0, 0))
    tall = pl.BlockSpec((1, width, D), lambda f: (f, 0, 0))
    total = parts * width
    return pl.pallas_call(
        ffn_kernel,
        grid=(parts,),
        in_specs=[whole, whole, wide, wide, tall],
        out_specs=[whole, whole, wide, wide, tall],
        out_shape=[
            jax.ShapeDtypeStruct((tok, D), f32),
            jax.ShapeDtypeStruct((tok, D), f32),
            jax.ShapeDtypeStruct(gate.shape, bf16),
            jax.ShapeDtypeStruct(gate.shape, bf16),
            jax.ShapeDtypeStruct(down.shape, bf16),
        ],
        scratch_shapes=[pltpu.VMEM((D, tok), bf16)],
        compiler_params=pltpu.CompilerParams(vmem_limit_bytes=VMEM_LIMIT),
        cost_estimate=pl.CostEstimate(
            flops=18 * tok * D * total, transcendentals=tok * total, bytes_accessed=12 * D * total
        ),
        name="feed_forward",
    )(x, c, gate, up, down)


def shards(
    inputs,
    encoded,
    doc_lengths,
    self_gain,
    self_query,
    self_key,
    self_value,
    self_output,
    bias_table,
    cross_gain,
    cross_query,
    cross_key,
    cross_value,
    cross_output,
    ffn_gain,
    ffn_gate,
    ffn_up,
    ffn_down,
    cotangent,
):
    count = lax.axis_size("ctx")
    owners = lax.axis_size("fsdp")
    parts = count // GROUPS
    lines = count // 2
    me = lax.axis_index("ctx")
    group, split = me // parts, me % parts
    line, side = me // 2, me % 2
    tok = inputs.shape[1]
    block = tok // parts
    length = count * tok
    rows = self_query.shape[0]

    swap = [(i, i ^ 1) for i in range(count)]
    ring = [(i, (i + 2) % count) for i in range(count)]

    def columns(w):
        return lax.dynamic_slice(w, (0, group * GL), (rows, GL))

    def as_row(v):
        v = v.reshape(1, -1)
        return jnp.pad(v, ((0, 0), (0, 3 * GL - v.shape[1])))

    packed = jnp.concatenate(
        [columns(self_query), columns(self_key), columns(self_value)], axis=1
    )
    packed = jnp.concatenate(
        [packed, as_row(jnp.concatenate([self_gain, cross_gain, ffn_gain])), as_row(bias_table)],
        axis=0,
    )
    packed = jnp.pad(packed, ((0, 14), (0, 0)))
    packed = lax.all_gather(packed, "fsdp", axis=0)
    w_qkv = packed[:, :rows].reshape(D, 3, GL)
    w_qkv = jnp.pad(w_qkv, ((0, 0), (0, 0), (0, GP - GL))).reshape(D, 3 * GP)
    gains = packed[:, rows, : 3 * rows].reshape(owners, 3, rows).transpose(1, 0, 2).reshape(3, D)
    gains = gains.astype(f32)
    gain_self, gain_cross, gain_ffn = gains[0], gains[1], gains[2]
    table_all = packed[:, rows + 1, : bias_table.size].reshape(NB, H).astype(f32)
    table = lax.dynamic_slice(table_all, (0, group * GH), (NB, GH))
    sizes = doc_lengths[0]
    ends = [sizes[0], sizes[0] + sizes[1], sizes[0] + sizes[1] + sizes[2]]
    meta = jnp.stack(ends + [split]).astype(jnp.int32)

    def project(x):
        v = x.astype(f32)
        normed = (v * inverse_rms(v) * gain_self).astype(bf16)
        return normed, matmul(normed, w_qkv).astype(bf16)

    normed_all = jnp.zeros((length, D), bf16)
    qkv = jnp.zeros((length, 3 * GP), bf16)
    piece = inputs[0]
    for s in range(lines):
        at = (line - s) % lines
        beside = lax.ppermute(piece, "ctx", swap)
        following = lax.ppermute(piece, "ctx", ring) if s + 1 < lines else None
        for x, owner in ((piece, 2 * at + side), (beside, 2 * at + 1 - side)):
            normed, projected = project(x)
            normed_all = lax.dynamic_update_slice(normed_all, normed, (owner * tok, 0))
            qkv = lax.dynamic_update_slice(qkv, projected, (owner * tok, 0))
        piece = following

    encoder = lax.all_gather(encoded[0], "ctx", axis=0, tiled=True)
    gather = lambda w: lax.all_gather(w, "fsdp", axis=0, tiled=True)
    w_output = gather(self_output)
    c_query = gather(cross_query)
    c_key = gather(cross_key)
    c_value = gather(cross_value)
    c_output = gather(cross_output)
    w_gate = lax.all_gather(ffn_gate, "fsdp", axis=0)
    w_up = lax.all_gather(ffn_up, "fsdp", axis=0)
    w_down = lax.all_gather(ffn_down, "fsdp", axis=0)

    out_chunks, self_full, lse = self_forward(qkv, meta, table, parts, count, tok)

    def to_owner(chunks):
        got = lax.all_to_all(chunks, "ctx", 0, 0, tiled=True)
        got = got.reshape(GROUPS, parts, block, GL)
        got = jnp.where(me % 2 == 0, got, got[:, ::-1])
        return got.transpose(1, 2, 0, 3).reshape(tok, D)

    def to_groups(x):
        got = x.reshape(parts, block, GROUPS, GL).transpose(2, 0, 1, 3)
        got = jnp.where(me % 2 == 0, got, got[:, ::-1])
        return lax.all_to_all(got.reshape(count, block, GL), "ctx", 0, 0, tiled=True)

    attended = to_owner(out_chunks)
    states = inputs[0].astype(f32)
    first_sum = states + matmul(attended, w_output)
    normed_two = (first_sum * inverse_rms(first_sum) * gain_cross).astype(bf16)
    cross_queries = matmul(normed_two, c_query).astype(bf16)
    cross_keys = matmul(encoder, c_key).astype(bf16)
    cross_values = matmul(encoder, c_value).astype(bf16)
    cross_out, cross_full, cross_lse = cross_forward(cross_queries, cross_keys, cross_values)
    second_sum = first_sum + matmul(cross_out, c_output)
    normed_three = (second_sum * inverse_rms(second_sum) * gain_ffn).astype(bf16)
    outer = cotangent[0]
    down_out, grad_three, d_gate, d_up, d_down = ffn(normed_three, outer, w_gate, w_up, w_down)
    outputs = (second_sum + down_out).astype(bf16)

    def reduce_weight(g):
        share = lax.psum_scatter(g, "fsdp", scatter_dimension=0, tiled=True)
        return lax.psum(share, "ctx").astype(f32)

    d_gate = reduce_weight(d_gate)[0]
    d_up = reduce_weight(d_up)[0]
    d_down = reduce_weight(d_down)[0]

    grad_part, grad_gain_ffn = norm_back(second_sum, gain_ffn, grad_three)
    grad_second = outer.astype(f32) + grad_part
    branch_two = grad_second.astype(bf16)
    grad_cross_out = right_matmul(branch_two, c_output).astype(bf16)
    grad_cq, grad_ck, grad_cv = cross_backward(
        cross_queries, cross_keys, cross_values, grad_cross_out, cross_full, cross_lse
    )
    grad_part, grad_gain_cross = norm_back(first_sum, gain_cross, right_matmul(grad_cq, c_query))
    grad_first = grad_second + grad_part
    branch_one = grad_first.astype(bf16)
    grad_attended = right_matmul(branch_one, w_output).astype(bf16)
    d_o = to_groups(grad_attended)
    d_o = jnp.pad(d_o, ((0, 0), (0, 0), (0, GP - GL)))

    d_c_output = reduce_weight(left_matmul(cross_out, branch_two).astype(bf16))
    d_c_query = reduce_weight(left_matmul(normed_two, grad_cq).astype(bf16))
    d_c_key = reduce_weight(left_matmul(encoder, grad_ck).astype(bf16))
    d_c_value = reduce_weight(left_matmul(encoder, grad_cv).astype(bf16))
    d_output = reduce_weight(left_matmul(attended, branch_one).astype(bf16))
    grad_enc = (right_matmul(grad_ck, c_key) + right_matmul(grad_cv, c_value)).astype(bf16)
    grad_enc = lax.psum_scatter(grad_enc, "ctx", scatter_dimension=0, tiled=True)

    d_qkv, table_rows = self_backward(qkv, meta, table, d_o, self_full, lse, parts, count, tok)

    def partial_at(at):
        return right_matmul(lax.dynamic_slice(d_qkv, (at * tok, 0), (tok, 3 * GP)), w_qkv)

    travelling = None
    for s in range(1, lines + 1):
        at = (line - s) % lines
        theirs = lax.ppermute(partial_at(2 * at + 1 - side).astype(bf16), "ctx", swap)
        both = partial_at(2 * at + side) + theirs.astype(f32)
        if travelling is not None:
            both = both + lax.ppermute(travelling.astype(bf16), "ctx", ring).astype(f32)
        travelling = both
    grad_one = travelling

    d_w = left_matmul(normed_all, d_qkv).reshape(D, 3, GP)[:, :, :GL].reshape(D, 3 * GL)
    d_w = lax.psum_scatter(d_w.astype(bf16), "fsdp", scatter_dimension=0, tiled=True)
    d_w = lax.all_gather(d_w, "ctx", axis=0)
    d_w = jnp.sum(d_w.astype(f32).reshape(GROUPS, parts, rows, 3, GL), axis=1)
    d_w = d_w.transpose(2, 1, 0, 3).reshape(3, rows, D)

    grad_part, grad_gain_self = norm_back(states, gain_self, grad_one)
    grad_states = (grad_first + grad_part).astype(bf16)

    grad_table = jnp.sum(table_rows, axis=1).reshape(GH, NB).T
    grad_table = lax.dynamic_update_slice(jnp.zeros((NB, H), f32), grad_table, (0, group * GH))
    small = jnp.concatenate(
        [grad_gain_self, grad_gain_cross, grad_gain_ffn, grad_table.reshape(-1)]
    )
    small = lax.psum(small, ("fsdp", "ctx"))
    owner = lax.axis_index("fsdp")
    own_gain = lambda k: lax.dynamic_slice(small, (k * D + owner * rows,), (rows,))
    own_table = lax.dynamic_slice(
        small[3 * D :].reshape(NB, H), (owner * (NB // owners), 0), (NB // owners, H)
    )
    return (
        outputs[None],
        grad_states[None],
        grad_enc[None],
        own_gain(0),
        d_w[0],
        d_w[1],
        d_w[2],
        d_output,
        own_table,
        own_gain(1),
        d_c_query,
        d_c_key,
        d_c_value,
        d_c_output,
        own_gain(2),
        d_gate,
        d_up,
        d_down,
    )


def solution(mesh):
    tokens = P("fsdp", "ctx", None)
    row = P("fsdp", None)
    col = P(None, "fsdp")
    vec = P("fsdp")
    in_specs = (
        (tokens, tokens, row, vec, row, row, row, row, row, vec, row, row, row, row, vec)
        + (col, col, row, tokens)
    )
    out_specs = (
        (tokens, tokens, tokens, vec, row, row, row, row, row, vec, row, row, row, row, vec)
        + (col, col, row)
    )
    return jax.shard_map(shards, mesh=mesh, in_specs=in_specs, out_specs=out_specs, check_vma=False)
```

```python
import functools
import math

import jax
import jax.numpy as jnp
from jax import lax
from jax.experimental import pallas as pl
from jax.experimental.pallas import tpu as pltpu
from jax.sharding import PartitionSpec as P

D = 768
H = 12
DH = 64
NB = 32
MAXD = 128
GROUPS = 4
GH = H // GROUPS
GL = GH * DH
GP = 256

epsilon = 1e-06
negative = -1e30
f32 = jnp.float32
bf16 = jnp.bfloat16
VMEM_LIMIT = 60 * 1024 * 1024


def thresholds():
    exact = NB // 2
    return list(range(1, exact + 1)) + [
        math.ceil(exact * (MAXD / exact) ** (t / exact)) for t in range(1, exact)
    ]


def matmul(a, b):
    return jnp.dot(a, b, preferred_element_type=f32)


def left_matmul(a, b):
    return lax.dot_general(a, b, (((0,), (0,)), ((), ())), preferred_element_type=f32)


def right_matmul(a, b):
    return lax.dot_general(a, b, (((1,), (1,)), ((), ())), preferred_element_type=f32)


def inverse_rms(v):
    return lax.rsqrt(jnp.mean(v * v, axis=-1, keepdims=True) + epsilon)


def norm_back(v, g, e):
    r = inverse_rms(v)
    ge = e * g
    grad_v = r * ge - v * (r * r * r * jnp.mean(ge * v, axis=-1, keepdims=True))
    return grad_v, jnp.sum(e * v * r, axis=0)


def flip(x):
    return x.astype(f32).T.astype(bf16)


def sub_of(i, split, parts):
    return jnp.where(i % 2 == 0, split, parts - 1 - split)


def doc_start(pos, meta):
    start = jnp.zeros_like(pos)
    for d in range(3):
        start = jnp.where(pos >= meta[d], meta[d], start)
    return start


def tile_bias(table, h, base, rows, cols):
    offset = base + (
        lax.broadcasted_iota(jnp.int32, (rows, cols), 1)
        - lax.broadcasted_iota(jnp.int32, (rows, cols), 0)
    )
    bias = jnp.full((rows, cols), table[0, h], f32)
    for b, at in enumerate(thresholds()):
        bias = jnp.where(offset >= at, table[b + 1, h], bias)
    return bias


def head_rows(x_t, h):
    parts = []
    if h:
        parts.append(jnp.zeros((h * DH, x_t.shape[1]), x_t.dtype))
    parts.append(x_t[h * DH : (h + 1) * DH])
    parts.append(jnp.zeros((GP - (h + 1) * DH, x_t.shape[1]), x_t.dtype))
    return jnp.concatenate(parts, axis=0)


def head_lanes(x, h):
    lane = lax.broadcasted_iota(jnp.int32, x.shape, 1)
    keep = (lane >= h * DH) & (lane < (h + 1) * DH)
    return jnp.where(keep, x.astype(f32), 0.0).astype(bf16)


def sweep(meta, first, block, step):
    start_lo = doc_start(first, meta)
    start_hi = doc_start(first + block - 1, meta)
    far_end = jnp.maximum(first // block - 1, 0)
    lo = jnp.minimum(start_lo // block, far_end)
    mid = jnp.clip((start_hi + block - 1) // block, lo, far_end)

    def masked(t, carry):
        step(pl.multiple_of(t * block, block), block, "masked")
        return carry

    lax.fori_loop(lo, mid, masked, 0)
    odd = (far_end - mid) % 2

    @pl.when(odd == 1)
    def _():
        step(pl.multiple_of(mid * block, block), block, "far")

    def far(t, carry):
        step(pl.multiple_of((mid + odd + 2 * t) * block, block), 2 * block, "far")
        return carry

    lax.fori_loop(0, (far_end - mid) // 2, far, 0)

    @pl.when(first > 0)
    def _():
        step(pl.multiple_of(jnp.maximum(first - block, 0), block), block, "prev")

    step(pl.multiple_of(first, block), block, "diag")


def tile_mask(kind, k0, rows, first, block, starts):
    key = k0 + lax.broadcasted_iota(jnp.int32, (rows, block), 0)
    mask = key >= starts
    if kind == "diag":
        query = first + lax.broadcasted_iota(jnp.int32, (rows, block), 1)
        mask = mask & (key <= query)
    return mask


def self_forward_kernel(
    parts, tok, meta, table, q_ref, k_ref, v_ref, o_ref, full_ref, lse_ref,
    v_t, bias, acc, top, total, q_masked,
):
    i = pl.program_id(0)
    block = tok // parts
    first = i * tok + sub_of(i, meta[3], parts) * block

    @pl.when(i == 0)
    def _():
        for h in range(GH):
            bias[h, 0] = tile_bias(table, h, 0, block, block)
            bias[h, 1] = tile_bias(table, h, block, block, block)

        def turn(t, carry):
            at = pl.multiple_of(t * block, block)
            v_t[:, pl.ds(at, block)] = flip(v_ref[pl.ds(at, block), :])
            return carry

        lax.fori_loop(0, v_ref.shape[0] // block, turn, 0)

    q_t = flip(q_ref[...])
    for h in range(GH):
        q_masked[h] = head_rows(q_t, h)
    top[...] = jnp.full_like(top, negative)
    total[...] = jnp.zeros_like(total)
    acc[...] = jnp.zeros_like(acc)
    starts = doc_start(first + lax.broadcasted_iota(jnp.int32, (1, block), 1), meta)

    def step(k0, rows, kind):
        k_tile = k_ref[pl.ds(k0, rows), :]
        if kind != "far":
            mask = tile_mask(kind, k0, rows, first, block, starts)
        for h in range(GH):
            s = matmul(k_tile, q_masked[h])
            shift = table[NB - 1, h]
            if kind == "diag":
                s, shift = s + bias[h, 0], 0.0
            elif kind == "prev":
                s, shift = s + bias[h, 1], 0.0
            if kind != "far":
                s = jnp.where(mask, s, negative)
            old = top[h : h + 1]
            new = jnp.maximum(old, jnp.max(s, axis=0, keepdims=True) + shift)
            scale = jnp.exp(old - new)
            p = jnp.exp(s - (new - shift))
            top[h : h + 1] = new
            total[h : h + 1] = total[h : h + 1] * scale + jnp.sum(p, axis=0, keepdims=True)
            rows_h = slice(h * DH, (h + 1) * DH)
            acc[rows_h] = acc[rows_h] * scale + matmul(
                v_t[rows_h, pl.ds(k0, rows)], p.astype(bf16)
            )

    sweep(meta, first, block, step)
    for h in range(GH):
        rows_h = slice(h * DH, (h + 1) * DH)
        acc[rows_h] = acc[rows_h] / total[h : h + 1]
    full_ref[...] = acc[:GL]
    o_ref[0] = acc[...].T[:, :GL].astype(bf16)
    lse_ref[...] = jnp.zeros_like(lse_ref)
    lse_ref[0:GH] = top[0:GH] + jnp.log(total[0:GH])


def self_backward_kernel(
    parts, tok, meta, table, q_ref, k_ref, v_ref, do_ref, full_ref, lse_ref, out_ref, tab_ref,
    k_t, bias, dk, dv, dq_t, near, far_sum, q_masked, do_masked, q_lanes, do_lanes, delta, do_wide,
):
    i = pl.program_id(0)
    block = tok // parts
    first = i * tok + sub_of(i, meta[3], parts) * block
    length = k_ref.shape[0]

    @pl.when(i == 0)
    def _():
        for h in range(GH):
            bias[h, 0] = tile_bias(table, h, 0, block, block)
            bias[h, 1] = tile_bias(table, h, block, block, block)
        near[...] = jnp.zeros_like(near)
        far_sum[...] = jnp.zeros_like(far_sum)
        do_wide[...] = jnp.zeros_like(do_wide)

        def turn(t, carry):
            at = pl.multiple_of(t * block, block)
            rows = pl.ds(at, block)
            k_t[:, rows] = flip(k_ref[rows, :])
            dk[rows, :] = jnp.zeros((block, GP), f32)
            dv[rows, :] = jnp.zeros((block, GP), f32)
            out_ref[rows, 0:GP] = jnp.zeros((block, GP), bf16)
            return carry

        lax.fori_loop(0, length // block, turn, 0)

    do_wide[:, :GL] = do_ref[0].astype(f32)
    do_full = do_wide[...]
    q_t = flip(q_ref[...])
    do_t = do_full.T
    for h in range(GH):
        rows_h = slice(h * DH, (h + 1) * DH)
        delta[h : h + 1] = jnp.sum(do_t[rows_h] * full_ref[rows_h], axis=0, keepdims=True)
        q_masked[h] = head_rows(q_t, h)
        do_masked[h] = head_rows(do_t.astype(bf16), h)
        q_lanes[h * block : (h + 1) * block] = head_lanes(q_ref[...], h)
        do_lanes[h * block : (h + 1) * block] = head_lanes(do_full, h)
    dq_t[...] = jnp.zeros_like(dq_t)
    starts = doc_start(first + lax.broadcasted_iota(jnp.int32, (1, block), 1), meta)

    def step(k0, rows, kind):
        at = pl.ds(k0, rows)
        k_tile = k_ref[at, :]
        v_tile = v_ref[at, :]
        if kind != "far":
            mask = tile_mask(kind, k0, rows, first, block, starts)
        probs, grads = [], []
        for h in range(GH):
            s = matmul(k_tile, q_masked[h])
            shift = lse_ref[h : h + 1]
            if kind == "diag":
                s = s + bias[h, 0]
            elif kind == "prev":
                s = s + bias[h, 1]
            else:
                shift = shift - table[NB - 1, h]
            p = jnp.exp(s - shift)
            if kind != "far":
                p = jnp.where(mask, p, 0.0)
            ds = p * (matmul(v_tile, do_masked[h]) - delta[h : h + 1])
            if kind == "diag":
                near[h, 0] += ds
            elif kind == "prev":
                near[h, 1] += ds
            else:
                far_sum[h : h + 1] += jnp.sum(ds, axis=0, keepdims=True)
            probs.append(p.astype(bf16))
            grads.append(ds.astype(bf16))
            rows_h = slice(h * DH, (h + 1) * DH)
            dq_t[rows_h] += matmul(k_t[rows_h, at], grads[h])
        dv[at, :] += matmul(jnp.concatenate(probs, axis=1), do_lanes[...])
        dk[at, :] += matmul(jnp.concatenate(grads, axis=1), q_lanes[...])

    sweep(meta, first, block, step)
    out_ref[pl.ds(pl.multiple_of(first, block), block), 0:GP] = dq_t[...].T.astype(bf16)

    @pl.when(i == pl.num_programs(0) - 1)
    def _():
        def emit(t, carry):
            rows = pl.ds(pl.multiple_of(t * block, block), block)
            out_ref[rows, GP : 2 * GP] = dk[rows, :].astype(bf16)
            out_ref[rows, 2 * GP : 3 * GP] = dv[rows, :].astype(bf16)
            return carry

        lax.fori_loop(0, length // block, emit, 0)
        offset = lax.broadcasted_iota(jnp.int32, (block, block), 1) - lax.broadcasted_iota(
            jnp.int32, (block, block), 0
        )
        edges = [None] + thresholds()
        for h in range(GH):
            tails = []
            for at in edges:
                if at is None:
                    part = near[h, 0] + near[h, 1]
                else:
                    part = jnp.where(offset >= at, near[h, 0], 0.0) + jnp.where(
                        offset + block >= at, near[h, 1], 0.0
                    )
                tails.append(jnp.sum(part, axis=0, keepdims=True))
            for b in range(NB):
                if b + 1 < NB:
                    row = tails[b] - tails[b + 1]
                else:
                    row = tails[b] + far_sum[h : h + 1]
                tab_ref[h * NB + b : h * NB + b + 1] = row


def self_specs(parts, tok, length):
    block = tok // parts
    q_spec = pl.BlockSpec((block, GP), lambda i, m: (i * parts + sub_of(i, m[3], parts), 0))
    k_spec = pl.BlockSpec((length, GP), lambda i, m: (0, 1), pipeline_mode=pl.Buffered(1))
    v_spec = pl.BlockSpec((length, GP), lambda i, m: (0, 2), pipeline_mode=pl.Buffered(1))
    table_spec = pl.BlockSpec(memory_space=pltpu.SMEM)
    return table_spec, q_spec, k_spec, v_spec


def pair_count(length):
    return GH * length * length // 8


def self_forward(qkv, meta, table, parts, count, tok):
    length = qkv.shape[0]
    block = tok // parts
    rows = count * block
    return pl.pallas_call(
        functools.partial(self_forward_kernel, parts, tok),
        grid_spec=pltpu.PrefetchScalarGridSpec(
            num_scalar_prefetch=1,
            grid=(count,),
            in_specs=list(self_specs(parts, tok, length)),
            out_specs=[
                pl.BlockSpec((1, block, GL), lambda i, m: (i, 0, 0)),
                pl.BlockSpec((GL, block), lambda i, m: (0, i)),
                pl.BlockSpec((8, block), lambda i, m: (0, i)),
            ],
            scratch_shapes=[
                pltpu.VMEM((GP, length), bf16),
                pltpu.VMEM((GH, 2, block, block), f32),
                pltpu.VMEM((GP, block), f32),
                pltpu.VMEM((8, block), f32),
                pltpu.VMEM((8, block), f32),
                pltpu.VMEM((GH, GP, block), bf16),
            ],
        ),
        out_shape=[
            jax.ShapeDtypeStruct((count, block, GL), bf16),
            jax.ShapeDtypeStruct((GL, rows), f32),
            jax.ShapeDtypeStruct((8, rows), f32),
        ],
        compiler_params=pltpu.CompilerParams(vmem_limit_bytes=VMEM_LIMIT),
        cost_estimate=pl.CostEstimate(
            flops=pair_count(length) * 1024,
            transcendentals=pair_count(length),
            bytes_accessed=length * GP * 8,
        ),
        name="self_forward",
    )(meta, table, qkv, qkv, qkv)


def self_backward(qkv, meta, table, d_o, full, lse, parts, count, tok):
    length = qkv.shape[0]
    block = tok // parts
    return pl.pallas_call(
        functools.partial(self_backward_kernel, parts, tok),
        grid_spec=pltpu.PrefetchScalarGridSpec(
            num_scalar_prefetch=1,
            grid=(count,),
            in_specs=list(self_specs(parts, tok, length))
            + [
                pl.BlockSpec((1, block, GL), lambda i, m: (i, 0, 0)),
                pl.BlockSpec((GL, block), lambda i, m: (0, i)),
                pl.BlockSpec((8, block), lambda i, m: (0, i)),
            ],
            out_specs=[
                pl.BlockSpec((length, 3 * GP), lambda i, m: (0, 0), pipeline_mode=pl.Buffered(1)),
                pl.BlockSpec((GH * NB, block), lambda i, m: (0, 0)),
            ],
            scratch_shapes=[
                pltpu.VMEM((GP, length), bf16),
                pltpu.VMEM((GH, 2, block, block), f32),
                pltpu.VMEM((length, GP), f32),
                pltpu.VMEM((length, GP), f32),
                pltpu.VMEM((GP, block), f32),
                pltpu.VMEM((GH, 2, block, block), f32),
                pltpu.VMEM((8, block), f32),
                pltpu.VMEM((GH, GP, block), bf16),
                pltpu.VMEM((GH, GP, block), bf16),
                pltpu.VMEM((GH * block, GP), bf16),
                pltpu.VMEM((GH * block, GP), bf16),
                pltpu.VMEM((8, block), f32),
                pltpu.VMEM((block, GP), f32),
            ],
        ),
        out_shape=[
            jax.ShapeDtypeStruct((length, 3 * GP), bf16),
            jax.ShapeDtypeStruct((GH * NB, block), f32),
        ],
        compiler_params=pltpu.CompilerParams(vmem_limit_bytes=VMEM_LIMIT),
        cost_estimate=pl.CostEstimate(
            flops=pair_count(length) * 2560,
            transcendentals=pair_count(length),
            bytes_accessed=length * GP * 16,
        ),
        name="self_backward",
    )(meta, table, qkv, qkv, qkv, d_o, full, lse)


PAIR = 2 * DH


def pair_rows(x_t, h):
    zeros = jnp.zeros((DH, x_t.shape[1]), x_t.dtype)
    own = x_t[h * DH : (h + 1) * DH]
    return jnp.concatenate([own, zeros] if h == 0 else [zeros, own], axis=0)


def cross_forward_kernel(q_ref, k_ref, v_ref, o_ref, full_ref, lse_ref, v_t, q_t):
    tok = q_ref.shape[0]
    chunk = math.gcd(tok, 256)
    v_t[...] = flip(v_ref[...])
    q_t[...] = flip(q_ref[...])
    lse_ref[...] = jnp.zeros_like(lse_ref)
    for at in range(0, tok, chunk):
        cols = slice(at, at + chunk)
        for h in range(2):
            rows_h = slice(h * DH, (h + 1) * DH)
            s = matmul(k_ref[...], pair_rows(q_t[:, cols], h))
            top = jnp.max(s, axis=0, keepdims=True)
            p = jnp.exp(s - top)
            total = jnp.sum(p, axis=0, keepdims=True)
            full_ref[rows_h, cols] = matmul(v_t[rows_h], p.astype(bf16)) / total
            lse_ref[h : h + 1, cols] = top + jnp.log(total)
    o_ref[...] = full_ref[...].T.astype(bf16)


def cross_backward_kernel(
    q_ref, k_ref, v_ref, do_ref, full_ref, lse_ref, dq_ref, dk_ref, dv_ref, k_t, q_t, do_t, dq_t,
    dk, dv,
):
    tok = q_ref.shape[0]
    chunk = math.gcd(tok, 256)
    k_t[...] = flip(k_ref[...])
    q_t[...] = flip(q_ref[...])
    do_t[...] = do_ref[...].astype(f32).T
    for at in range(0, tok, chunk):
        cols = slice(at, at + chunk)
        probs, grads, q_lanes, do_lanes = [], [], [], []
        for h in range(2):
            rows_h = slice(h * DH, (h + 1) * DH)
            s = matmul(k_ref[...], pair_rows(q_t[:, cols], h))
            p = jnp.exp(s - lse_ref[h : h + 1, cols])
            delta = jnp.sum(do_t[rows_h, cols] * full_ref[rows_h, cols], axis=0, keepdims=True)
            dp = matmul(v_ref[...], pair_rows(do_t[:, cols].astype(bf16), h))
            ds = (p * (dp - delta)).astype(bf16)
            probs.append(p.astype(bf16))
            grads.append(ds)
            dq_t[rows_h, cols] = matmul(k_t[rows_h], ds)
            q_lanes.append(head_lanes(q_ref[cols, :], h))
            do_lanes.append(head_lanes(do_ref[cols, :], h))
        part_v = matmul(jnp.concatenate(probs, axis=1), jnp.concatenate(do_lanes, axis=0))
        part_k = matmul(jnp.concatenate(grads, axis=1), jnp.concatenate(q_lanes, axis=0))
        if at == 0:
            dv[...] = part_v
            dk[...] = part_k
        else:
            dv[...] += part_v
            dk[...] += part_k
    dq_ref[...] = dq_t[...].T.astype(bf16)
    dk_ref[...] = dk[...].astype(bf16)
    dv_ref[...] = dv[...].astype(bf16)


def cross_forward(q, k, v):
    tok, enc = q.shape[0], k.shape[0]
    pairs = H // 2
    col = lambda p: (0, p)
    row = lambda p: (p, 0)
    return pl.pallas_call(
        cross_forward_kernel,
        grid=(pairs,),
        in_specs=[
            pl.BlockSpec((tok, PAIR), col),
            pl.BlockSpec((enc, PAIR), col),
            pl.BlockSpec((enc, PAIR), col),
        ],
        out_specs=[
            pl.BlockSpec((tok, PAIR), col),
            pl.BlockSpec((PAIR, tok), row),
            pl.BlockSpec((8, tok), row),
        ],
        out_shape=[
            jax.ShapeDtypeStruct((tok, D), bf16),
            jax.ShapeDtypeStruct((D, tok), f32),
            jax.ShapeDtypeStruct((8 * pairs, tok), f32),
        ],
        scratch_shapes=[pltpu.VMEM((PAIR, enc), bf16), pltpu.VMEM((PAIR, tok), bf16)],
        compiler_params=pltpu.CompilerParams(vmem_limit_bytes=VMEM_LIMIT),
        cost_estimate=pl.CostEstimate(
            flops=H * tok * enc * 1024, transcendentals=H * tok * enc, bytes_accessed=D * tok * 12
        ),
        name="cross_forward",
    )(q, k, v)


def cross_backward(q, k, v, d_o, full, lse):
    tok, enc = q.shape[0], k.shape[0]
    pairs = H // 2
    col = lambda p: (0, p)
    row = lambda p: (p, 0)
    return pl.pallas_call(
        cross_backward_kernel,
        grid=(pairs,),
        in_specs=[
            pl.BlockSpec((tok, PAIR), col),
            pl.BlockSpec((enc, PAIR), col),
            pl.BlockSpec((enc, PAIR), col),
            pl.BlockSpec((tok, PAIR), col),
            pl.BlockSpec((PAIR, tok), row),
            pl.BlockSpec((8, tok), row),
        ],
        out_specs=[
            pl.BlockSpec((tok, PAIR), col),
            pl.BlockSpec((enc, PAIR), col),
            pl.BlockSpec((enc, PAIR), col),
        ],
        out_shape=[
            jax.ShapeDtypeStruct((tok, D), bf16),
            jax.ShapeDtypeStruct((enc, D), bf16),
            jax.ShapeDtypeStruct((enc, D), bf16),
        ],
        scratch_shapes=[
            pltpu.VMEM((PAIR, enc), bf16),
            pltpu.VMEM((PAIR, tok), bf16),
            pltpu.VMEM((PAIR, tok), f32),
            pltpu.VMEM((PAIR, tok), f32),
            pltpu.VMEM((enc, PAIR), f32),
            pltpu.VMEM((enc, PAIR), f32),
        ],
        compiler_params=pltpu.CompilerParams(vmem_limit_bytes=VMEM_LIMIT),
        cost_estimate=pl.CostEstimate(
            flops=H * tok * enc * 2560, transcendentals=H * tok * enc, bytes_accessed=D * tok * 20
        ),
        name="cross_backward",
    )(q, k, v, d_o, full, lse)


LANES = 128


def gelu_pair(v):
    inner = math.sqrt(2 / math.pi) * (v + 0.044715 * (v * v * v))
    t = jnp.tanh(inner)
    half = 0.5 * (1.0 + t)
    slope = half + 0.5 * v * (1.0 - t * t) * (
        math.sqrt(2 / math.pi) * (1.0 + 3 * 0.044715 * (v * v))
    )
    return v * half, slope


def ffn_kernel(
    x_ref, c_ref, gate_ref, up_ref, down_ref, out_ref, gx_ref, dw_ref, x_t
):
    f = pl.program_id(0)

    @pl.when(f == 0)
    def _():
        x_t[...] = flip(x_ref[...])
        out_ref[...] = jnp.zeros_like(out_ref)
        gx_ref[...] = jnp.zeros_like(gx_ref)

    def emit(g, at):
        for lane in range(0, g.shape[1], LANES):
            dw_ref[0, 0, at : at + g.shape[0]] = g[:, lane : lane + LANES].astype(bf16)
            at += g.shape[0]
        return at

    x = x_ref[...]
    c = c_ref[...]
    w_gate, w_up, w_down = gate_ref[0], up_ref[0], down_ref[0]
    gate = matmul(x, w_gate)
    up = matmul(x, w_up)
    act, slope = gelu_pair(gate)
    hidden_full = act * up
    hidden = hidden_full.astype(bf16)
    out_ref[...] += matmul(hidden, w_down)
    grad_hidden = right_matmul(c, w_down)
    at = emit(matmul(flip(hidden), c), 0)
    grad_gate = (grad_hidden * up * slope).astype(bf16)
    grad_up = (grad_hidden * act).astype(bf16)
    at = emit(matmul(x_t[...], grad_gate), at)
    at = emit(matmul(x_t[...], grad_up), at)
    gx_ref[...] += right_matmul(grad_gate, w_gate) + right_matmul(grad_up, w_up)


def ffn(x, c, gate, up, down):
    tok = x.shape[0]
    parts, _, width = gate.shape
    whole = pl.BlockSpec((tok, D), lambda f: (0, 0))
    wide = pl.BlockSpec((1, D, width), lambda f: (f, 0, 0))
    tall = pl.BlockSpec((1, width, D), lambda f: (f, 0, 0))
    total = parts * width
    lines = 3 * D * width // LANES
    return pl.pallas_call(
        ffn_kernel,
        grid=(parts,),
        in_specs=[whole, whole, wide, wide, tall],
        out_specs=[
            whole,
            whole,
            pl.BlockSpec((1, 1, lines, LANES), lambda f: (f % 2, f // 2, 0, 0)),
        ],
        out_shape=[
            jax.ShapeDtypeStruct((tok, D), f32),
            jax.ShapeDtypeStruct((tok, D), f32),
            jax.ShapeDtypeStruct((2, parts // 2, lines, LANES), bf16),
        ],
        scratch_shapes=[pltpu.VMEM((D, tok), bf16)],
        compiler_params=pltpu.CompilerParams(vmem_limit_bytes=VMEM_LIMIT),
        cost_estimate=pl.CostEstimate(
            flops=18 * tok * D * total, transcendentals=tok * total, bytes_accessed=12 * D * total
        ),
        name="feed_forward",
    )(x, c, gate, up, down)


def split_ffn(flat, width):
    down = flat[: 6 * width].reshape(6, width, LANES)
    rest = flat[6 * width :].reshape(2, width // LANES, D, LANES)
    join = lambda x: jnp.concatenate([x[i] for i in range(x.shape[0])], axis=1)
    return join(rest[0]), join(rest[1]), join(down)


def weights_kernel(rows, *refs):
    out_ref = refs[-1]
    for i in range(len(refs) // 2):
        g = matmul(flip(refs[2 * i][...]), refs[2 * i + 1][...]).astype(bf16)
        for f in range(D // rows):
            out_ref[f % 2, f // 2, i * rows : (i + 1) * rows] = g[f * rows : (f + 1) * rows]


def weight_grads(pairs, rows):
    count = len(pairs)
    owners = D // rows
    flat = [x for pair in pairs for x in pair]
    return pl.pallas_call(
        functools.partial(weights_kernel, rows),
        out_shape=jax.ShapeDtypeStruct((2, owners // 2, count * rows, D), bf16),
        compiler_params=pltpu.CompilerParams(vmem_limit_bytes=VMEM_LIMIT),
        cost_estimate=pl.CostEstimate(
            flops=sum(2 * D * D * x.shape[0] for x, _ in pairs),
            transcendentals=0,
            bytes_accessed=sum(x.size * 2 for x in flat) + 2 * count * D * D,
        ),
        name="weight_grads",
    )(*flat)


def shards(
    inputs,
    encoded,
    doc_lengths,
    self_gain,
    self_query,
    self_key,
    self_value,
    self_output,
    bias_table,
    cross_gain,
    cross_query,
    cross_key,
    cross_value,
    cross_output,
    ffn_gain,
    ffn_gate,
    ffn_up,
    ffn_down,
    cotangent,
):
    count = lax.axis_size("ctx")
    owners = lax.axis_size("fsdp")
    parts = count // GROUPS
    lines = count // 2
    me = lax.axis_index("ctx")
    group, split = me // parts, me % parts
    line, side = me // 2, me % 2
    tok = inputs.shape[1]
    enc = encoded.shape[1]
    block = tok // parts
    half = owners // 2
    owner_me = lax.axis_index("fsdp")
    core = owner_me % 2
    length = count * tok
    rows = self_query.shape[0]

    swap = [(i, i ^ 1) for i in range(count)]
    ring = [(i, (i + 2) % count) for i in range(count)]

    def columns(w):
        return lax.dynamic_slice(w, (0, group * GL), (rows, GL))

    def as_row(v):
        v = v.reshape(1, -1)
        return jnp.pad(v, ((0, 0), (0, 3 * GL - v.shape[1])))

    packed = jnp.concatenate(
        [columns(self_query), columns(self_key), columns(self_value)], axis=1
    )
    packed = jnp.concatenate(
        [packed, as_row(jnp.concatenate([self_gain, cross_gain, ffn_gain])), as_row(bias_table)],
        axis=0,
    )
    packed = jnp.pad(packed, ((0, 14), (0, 0)))
    packed = lax.all_gather(packed, "fsdp", axis=0)
    w_qkv = packed[:, :rows].reshape(D, 3, GL)
    w_qkv = jnp.pad(w_qkv, ((0, 0), (0, 0), (0, GP - GL))).reshape(D, 3 * GP)
    gains = packed[:, rows, : 3 * rows].reshape(owners, 3, rows).transpose(1, 0, 2).reshape(3, D)
    gains = gains.astype(f32)
    gain_self, gain_cross, gain_ffn = gains[0], gains[1], gains[2]
    table_all = packed[:, rows + 1, : bias_table.size].reshape(NB, H).astype(f32)
    table = lax.dynamic_slice(table_all, (0, group * GH), (NB, GH))
    sizes = doc_lengths[0]
    ends = [sizes[0], sizes[0] + sizes[1], sizes[0] + sizes[1] + sizes[2]]
    meta = jnp.stack(ends + [split]).astype(jnp.int32)

    def project(x):
        v = x.astype(f32)
        normed = (v * inverse_rms(v) * gain_self).astype(bf16)
        return normed, matmul(normed, w_qkv).astype(bf16)

    normed_all = jnp.zeros((length, D), bf16)
    qkv = jnp.zeros((length, 3 * GP), bf16)
    encoder = jnp.zeros((count * enc, D), bf16)
    piece = jnp.concatenate([inputs[0], encoded[0]], axis=0)
    for s in range(lines):
        at = (line - s) % lines
        beside = lax.ppermute(piece, "ctx", swap)
        following = lax.ppermute(piece, "ctx", ring) if s + 1 < lines else None
        for x, owner in ((piece, 2 * at + side), (beside, 2 * at + 1 - side)):
            normed, projected = project(x[:tok])
            encoder = lax.dynamic_update_slice(encoder, x[tok:], (owner * enc, 0))
            normed_all = lax.dynamic_update_slice(normed_all, normed, (owner * tok, 0))
            qkv = lax.dynamic_update_slice(qkv, projected, (owner * tok, 0))
        piece = following

    gather = lambda w: lax.all_gather(w, "fsdp", axis=0, tiled=True)
    w_output = gather(self_output)
    c_query = gather(cross_query)
    c_key = gather(cross_key)
    c_value = gather(cross_value)
    c_output = gather(cross_output)
    w_gate = lax.all_gather(ffn_gate, "fsdp", axis=0)
    w_up = lax.all_gather(ffn_up, "fsdp", axis=0)
    w_down = lax.all_gather(ffn_down, "fsdp", axis=0)

    out_chunks, self_full, lse = self_forward(qkv, meta, table, parts, count, tok)

    def turned(x):
        even = me % 2 == 0
        return jnp.stack(
            [jnp.where(even, x[:, s], x[:, parts - 1 - s]) for s in range(parts)], axis=1
        )

    def to_owner(chunks):
        got = lax.all_to_all(chunks, "ctx", 0, 0, tiled=True)
        got = got.reshape(GROUPS, parts, block, GL)
        return turned(got).transpose(1, 2, 0, 3).reshape(tok, D)

    def to_groups(x):
        got = x.reshape(GROUPS, parts, block, GL)
        got = turned(got)
        return lax.all_to_all(got.reshape(count, block, GL), "ctx", 0, 0, tiled=True)

    core_pairs = [(i, i ^ 1) for i in range(owners)]
    core_groups = [[b + 2 * i for i in range(half)] for b in range(2)]
    group_groups = [[g * parts + s for g in range(GROUPS)] for s in range(parts)]

    def add_up(x):
        return jnp.sum(x.astype(f32), axis=0)

    def pick(g, i, axis=0):
        return lax.dynamic_index_in_dim(g, i, axis, keepdims=False)

    def swap_cores(g, axis=0):
        got = lax.ppermute(pick(g, 1 - core, axis), "fsdp", core_pairs)
        return (pick(g, core, axis).astype(f32) + got.astype(f32)).astype(bf16)

    def over_chips(g):
        chip = owner_me // 2
        got = [pick(g, chip)]
        for k in range(1, half):
            route = [(i, (i // 2 + k) % half * 2 + i % 2) for i in range(owners)]
            got.append(lax.ppermute(pick(g, (chip + k) % half), "fsdp", route))
        return got

    def over_splits(g):
        got = [g]
        for k in range(1, parts):
            route = [(i, i // parts * parts + (i % parts + k) % parts) for i in range(count)]
            got.append(lax.ppermute(g, "ctx", route))
        return got

    def total(got):
        return sum(x.astype(f32) for x in got)

    def over_ctx(g):
        g = g.astype(bf16).reshape(count, g.shape[0] // count, g.shape[1])
        return lax.all_to_all(g, "ctx", 0, 0, tiled=True)

    def over_groups(g):
        g = jnp.broadcast_to(g[None], (GROUPS,) + g.shape)
        return lax.all_to_all(g, "ctx", 0, 0, tiled=True, axis_index_groups=group_groups)

    def whole(g):
        return lax.all_gather(g.astype(bf16), "ctx", axis=0, tiled=True).astype(f32)

    attended = to_owner(out_chunks)
    states = inputs[0].astype(f32)
    first_sum = states + matmul(attended, w_output)
    normed_two = (first_sum * inverse_rms(first_sum) * gain_cross).astype(bf16)
    cross_queries = matmul(normed_two, c_query).astype(bf16)
    cross_keys = matmul(encoder, c_key).astype(bf16)
    cross_values = matmul(encoder, c_value).astype(bf16)
    cross_out, cross_full, cross_lse = cross_forward(cross_queries, cross_keys, cross_values)
    second_sum = first_sum + matmul(cross_out, c_output)
    normed_three = (second_sum * inverse_rms(second_sum) * gain_ffn).astype(bf16)
    outer = cotangent[0]
    down_out, grad_three, d_ffn = ffn(normed_three, outer, w_gate, w_up, w_down)
    outputs = (second_sum + down_out).astype(bf16)
    d_ffn = over_chips(swap_cores(d_ffn))

    grad_part, grad_gain_ffn = norm_back(second_sum, gain_ffn, grad_three)
    grad_second = outer.astype(f32) + grad_part
    branch_two = grad_second.astype(bf16)
    grad_cross_out = right_matmul(branch_two, c_output).astype(bf16)
    grad_cq, grad_ck, grad_cv = cross_backward(
        cross_queries, cross_keys, cross_values, grad_cross_out, cross_full, cross_lse
    )
    grad_part, grad_gain_cross = norm_back(first_sum, gain_cross, right_matmul(grad_cq, c_query))
    grad_first = grad_second + grad_part
    branch_one = grad_first.astype(bf16)
    grad_attended = jnp.einsum(
        "td,gcd->gtc", branch_one, w_output.reshape(GROUPS, GL, D), preferred_element_type=f32
    ).astype(bf16)
    d_o = to_groups(grad_attended)
    grad_enc = (right_matmul(grad_ck, c_key) + right_matmul(grad_cv, c_value)).astype(bf16)
    d_rest = swap_cores(
        weight_grads(
            [
                (attended, branch_one),
                (normed_two, grad_cq),
                (encoder, grad_ck),
                (encoder, grad_cv),
                (cross_out, branch_two),
            ],
            rows,
        )
    )
    grad_enc = over_ctx(grad_enc)
    d_ffn = total(d_ffn).astype(bf16)
    d_o, d_ffn, d_rest, grad_enc = lax.optimization_barrier((d_o, d_ffn, d_rest, grad_enc))

    d_ffn = over_ctx(d_ffn)
    d_rest = over_chips(d_rest)
    d_qkv, table_rows = self_backward(qkv, meta, table, d_o, self_full, lse, parts, count, tok)
    d_qkv, d_ffn, d_rest = lax.optimization_barrier((d_qkv, d_ffn, d_rest))

    grad_enc = add_up(grad_enc).astype(bf16)
    d_gate, d_up, d_down = split_ffn(whole(add_up(d_ffn)), ffn_gate.shape[1])
    d_rest = whole(add_up(over_ctx(total(d_rest))))
    d_rest = [d_rest[i * rows : (i + 1) * rows] for i in range(5)]
    d_output, d_c_query, d_c_key, d_c_value, d_c_output = d_rest

    d_w = left_matmul(normed_all, d_qkv).astype(bf16).reshape(owners, rows, 3 * GP)
    wide = lambda x: jnp.pad(x, ((0, 0), (0, 3 * GP - x.shape[1])))
    table_part = jnp.sum(table_rows, axis=1)[None]
    gain_part = jnp.stack([grad_gain_cross, grad_gain_ffn]).reshape(2, owners, rows)
    extra = jnp.stack(
        [
            jnp.broadcast_to(wide(table_part), (owners, 3 * GP)),
            wide(gain_part[0]),
            wide(gain_part[1]),
        ],
        axis=1,
    )
    extra = jnp.pad(extra, ((0, 0), (0, 13), (0, 0))).astype(bf16)
    d_w = jnp.concatenate([d_w, extra], axis=1)
    d_w = swap_cores(d_w.reshape((half, 2) + d_w.shape[1:]), 1)
    d_w = total(over_chips(d_w)).astype(bf16)
    d_w = total(over_splits(d_w)).astype(bf16)
    d_w = over_groups(d_w).astype(f32)
    grad_table = d_w[:, rows, : GH * NB].reshape(H, NB).T
    grad_gain_cross = jnp.sum(d_w[:, rows + 1, :rows], axis=0)
    grad_gain_ffn = jnp.sum(d_w[:, rows + 2, :rows], axis=0)
    d_w = [
        jnp.concatenate([d_w[g, :rows, i * GP : i * GP + GL] for g in range(GROUPS)], axis=1)
        for i in range(3)
    ]
    grad_gain_self = sum(
        jnp.sum(w.astype(f32) * d, axis=1)
        for w, d in zip((self_query, self_key, self_value), d_w)
    ) / self_gain.astype(f32)

    def partial_at(at):
        return right_matmul(lax.dynamic_slice(d_qkv, (at * tok, 0), (tok, 3 * GP)), w_qkv)

    travelling = None
    for s in range(1, lines + 1):
        at = (line - s) % lines
        theirs = lax.ppermute(partial_at(2 * at + 1 - side).astype(bf16), "ctx", swap)
        both = partial_at(2 * at + side) + theirs.astype(f32)
        if travelling is not None:
            both = both + lax.ppermute(travelling.astype(bf16), "ctx", ring).astype(f32)
        travelling = both
    grad_one = travelling

    grad_part, _ = norm_back(states, gain_self, grad_one)
    grad_states = (grad_first + grad_part).astype(bf16)
    own_table = lax.dynamic_slice(
        grad_table, (owner_me * (NB // owners), 0), (NB // owners, H)
    )
    return (
        outputs[None],
        grad_states[None],
        grad_enc[None],
        grad_gain_self,
        d_w[0],
        d_w[1],
        d_w[2],
        d_output,
        own_table,
        grad_gain_cross,
        d_c_query,
        d_c_key,
        d_c_value,
        d_c_output,
        grad_gain_ffn,
        d_gate,
        d_up,
        d_down,
    )


def solution(mesh):
    tokens = P("fsdp", "ctx", None)
    row = P("fsdp", None)
    col = P(None, "fsdp")
    vec = P("fsdp")
    in_specs = (
        (tokens, tokens, row, vec, row, row, row, row, row, vec, row, row, row, row, vec)
        + (col, col, row, tokens)
    )
    out_specs = (
        (tokens, tokens, tokens, vec, row, row, row, row, row, vec, row, row, row, row, vec)
        + (col, col, row)
    )
    return jax.shard_map(shards, mesh=mesh, in_specs=in_specs, out_specs=out_specs, check_vma=False)
```

```python
import functools
import math

import jax
import jax.numpy as jnp
from jax import lax
from jax.experimental import pallas as pl
from jax.experimental.pallas import tpu as pltpu
from jax.sharding import PartitionSpec as P

D = 768
H = 12
DH = 64
NB = 32
MAXD = 128
GROUPS = 4
GH = H // GROUPS
GL = GH * DH
GP = 256

epsilon = 1e-06
negative = -1e30
f32 = jnp.float32
bf16 = jnp.bfloat16
VMEM_LIMIT = 60 * 1024 * 1024


def thresholds():
    exact = NB // 2
    return list(range(1, exact + 1)) + [
        math.ceil(exact * (MAXD / exact) ** (t / exact)) for t in range(1, exact)
    ]


def matmul(a, b):
    return jnp.dot(a, b, preferred_element_type=f32)


def left_matmul(a, b):
    return lax.dot_general(a, b, (((0,), (0,)), ((), ())), preferred_element_type=f32)


def right_matmul(a, b):
    return lax.dot_general(a, b, (((1,), (1,)), ((), ())), preferred_element_type=f32)


def inverse_rms(v):
    return lax.rsqrt(jnp.mean(v * v, axis=-1, keepdims=True) + epsilon)


def norm_back(v, g, e):
    r = inverse_rms(v)
    ge = e * g
    grad_v = r * ge - v * (r * r * r * jnp.mean(ge * v, axis=-1, keepdims=True))
    return grad_v, jnp.sum(e * v * r, axis=0)


def fold(x, op):
    while x.shape[0] > 8:
        half = x.shape[0] // 2
        x = op(x[:half], x[half:])
    reduce = jnp.max if op is jnp.maximum else jnp.sum
    return reduce(x, axis=0, keepdims=True)


def flip(x):
    return x.astype(f32).T.astype(bf16)


def sub_of(i, split, parts):
    return jnp.where(i % 2 == 0, split, parts - 1 - split)


def doc_start(pos, meta):
    start = jnp.zeros_like(pos)
    for d in range(3):
        start = jnp.where(pos >= meta[d], meta[d], start)
    return start


def tile_bias(table, h, base, rows, cols):
    offset = base + (
        lax.broadcasted_iota(jnp.int32, (rows, cols), 1)
        - lax.broadcasted_iota(jnp.int32, (rows, cols), 0)
    )
    bias = jnp.full((rows, cols), table[0, h], f32)
    for b, at in enumerate(thresholds()):
        bias = jnp.where(offset >= at, table[b + 1, h], bias)
    return bias


def head_rows(x_t, h):
    parts = []
    if h:
        parts.append(jnp.zeros((h * DH, x_t.shape[1]), x_t.dtype))
    parts.append(x_t[h * DH : (h + 1) * DH])
    parts.append(jnp.zeros((GP - (h + 1) * DH, x_t.shape[1]), x_t.dtype))
    return jnp.concatenate(parts, axis=0)


def head_lanes(x, h):
    lane = lax.broadcasted_iota(jnp.int32, x.shape, 1)
    keep = (lane >= h * DH) & (lane < (h + 1) * DH)
    return jnp.where(keep, x.astype(f32), 0.0).astype(bf16)


def sweep(meta, first, block, step):
    start_lo = doc_start(first, meta)
    start_hi = doc_start(first + block - 1, meta)
    far_end = jnp.maximum(first // block - 1, 0)
    lo = jnp.minimum(start_lo // block, far_end)
    mid = jnp.clip((start_hi + block - 1) // block, lo, far_end)

    def masked(t, carry):
        step(pl.multiple_of(t * block, block), block, "masked")
        return carry

    lax.fori_loop(lo, mid, masked, 0)
    odd = (far_end - mid) % 2

    @pl.when(odd == 1)
    def _():
        step(pl.multiple_of(mid * block, block), block, "far")

    def far(t, carry):
        step(pl.multiple_of((mid + odd + 2 * t) * block, block), 2 * block, "far")
        return carry

    lax.fori_loop(0, (far_end - mid) // 2, far, 0)

    @pl.when(first > 0)
    def _():
        step(pl.multiple_of(jnp.maximum(first - block, 0), block), block, "prev")

    step(pl.multiple_of(first, block), block, "diag")


def tile_mask(kind, k0, rows, first, block, starts):
    key = k0 + lax.broadcasted_iota(jnp.int32, (rows, block), 0)
    mask = key >= starts
    if kind == "diag":
        query = first + lax.broadcasted_iota(jnp.int32, (rows, block), 1)
        mask = mask & (key <= query)
    return mask


def self_forward_kernel(
    parts, tok, meta, table, q_ref, k_ref, v_ref, o_ref, full_ref, lse_ref,
    v_t, bias, acc, top, total, q_masked,
):
    i = pl.program_id(0)
    block = tok // parts
    first = i * tok + sub_of(i, meta[3], parts) * block

    @pl.when(i == 0)
    def _():
        for h in range(GH):
            bias[h, 0] = tile_bias(table, h, 0, block, block)
            bias[h, 1] = tile_bias(table, h, block, block, block)

        def turn(t, carry):
            at = pl.multiple_of(t * block, block)
            v_t[:, pl.ds(at, block)] = flip(v_ref[pl.ds(at, block), :])
            return carry

        lax.fori_loop(0, v_ref.shape[0] // block, turn, 0)

    q_t = flip(q_ref[...])
    for h in range(GH):
        q_masked[h] = head_rows(q_t, h)
    top[...] = jnp.full_like(top, negative)
    total[...] = jnp.zeros_like(total)
    acc[...] = jnp.zeros_like(acc)
    starts = doc_start(first + lax.broadcasted_iota(jnp.int32, (1, block), 1), meta)

    def step(k0, rows, kind):
        k_tile = k_ref[pl.ds(k0, rows), :]
        if kind != "far":
            mask = tile_mask(kind, k0, rows, first, block, starts)
        all_scores = [matmul(k_tile, q_masked[h]) for h in range(GH)]
        probs, scales = [], []
        for h in range(GH):
            s = all_scores[h]
            shift = table[NB - 1, h]
            if kind == "diag":
                s, shift = s + bias[h, 0], 0.0
            elif kind == "prev":
                s, shift = s + bias[h, 1], 0.0
            if kind != "far":
                s = jnp.where(mask, s, negative)
            old = top[h : h + 1]
            new = jnp.maximum(old, fold(s, jnp.maximum) + shift)
            scale = jnp.exp(old - new)
            p = jnp.exp(s - (new - shift))
            top[h : h + 1] = new
            total[h : h + 1] = total[h : h + 1] * scale + fold(p, jnp.add)
            probs.append(p.astype(bf16))
            scales.append(scale)
        for h in range(GH):
            rows_h = slice(h * DH, (h + 1) * DH)
            acc[rows_h] = acc[rows_h] * scales[h] + matmul(v_t[rows_h, pl.ds(k0, rows)], probs[h])

    sweep(meta, first, block, step)
    for h in range(GH):
        rows_h = slice(h * DH, (h + 1) * DH)
        acc[rows_h] = acc[rows_h] / total[h : h + 1]
    full_ref[...] = acc[:GL]
    o_ref[0] = acc[...].T[:, :GL].astype(bf16)
    lse_ref[...] = jnp.zeros_like(lse_ref)
    lse_ref[0:GH] = top[0:GH] + jnp.log(total[0:GH])


def self_backward_kernel(
    parts, tok, meta, table, q_ref, k_ref, v_ref, do_ref, full_ref, lse_ref, out_ref, tab_ref,
    k_t, bias, dk, dv, dq_t, near, far_sum, q_masked, do_masked, q_lanes, do_lanes, delta, do_wide,
):
    i = pl.program_id(0)
    block = tok // parts
    first = i * tok + sub_of(i, meta[3], parts) * block
    length = k_ref.shape[0]

    @pl.when(i == 0)
    def _():
        for h in range(GH):
            bias[h, 0] = tile_bias(table, h, 0, block, block)
            bias[h, 1] = tile_bias(table, h, block, block, block)
        near[...] = jnp.zeros_like(near)
        far_sum[...] = jnp.zeros_like(far_sum)
        do_wide[...] = jnp.zeros_like(do_wide)

        def turn(t, carry):
            at = pl.multiple_of(t * block, block)
            rows = pl.ds(at, block)
            k_t[:, rows] = flip(k_ref[rows, :])
            dk[rows, :] = jnp.zeros((block, GP), f32)
            dv[rows, :] = jnp.zeros((block, GP), f32)
            out_ref[rows, 0:GP] = jnp.zeros((block, GP), bf16)
            return carry

        lax.fori_loop(0, length // block, turn, 0)

    do_wide[:, :GL] = do_ref[0].astype(f32)
    do_full = do_wide[...]
    q_t = flip(q_ref[...])
    do_t = do_full.T
    for h in range(GH):
        rows_h = slice(h * DH, (h + 1) * DH)
        delta[h : h + 1] = jnp.sum(do_t[rows_h] * full_ref[rows_h], axis=0, keepdims=True)
        q_masked[h] = head_rows(q_t, h)
        do_masked[h] = head_rows(do_t.astype(bf16), h)
        q_lanes[h * block : (h + 1) * block] = head_lanes(q_ref[...], h)
        do_lanes[h * block : (h + 1) * block] = head_lanes(do_full, h)
    dq_t[...] = jnp.zeros_like(dq_t)
    starts = doc_start(first + lax.broadcasted_iota(jnp.int32, (1, block), 1), meta)

    def step(k0, rows, kind):
        at = pl.ds(k0, rows)
        k_tile = k_ref[at, :]
        v_tile = v_ref[at, :]
        if kind != "far":
            mask = tile_mask(kind, k0, rows, first, block, starts)
        probs, grads = [], []
        for h in range(GH):
            s = matmul(k_tile, q_masked[h])
            shift = lse_ref[h : h + 1]
            if kind == "diag":
                s = s + bias[h, 0]
            elif kind == "prev":
                s = s + bias[h, 1]
            else:
                shift = shift - table[NB - 1, h]
            p = jnp.exp(s - shift)
            if kind != "far":
                p = jnp.where(mask, p, 0.0)
            ds = p * (matmul(v_tile, do_masked[h]) - delta[h : h + 1])
            if kind == "diag":
                near[h, 0] += ds
            elif kind == "prev":
                near[h, 1] += ds
            else:
                far_sum[h : h + 1] += fold(ds, jnp.add)
            probs.append(p.astype(bf16))
            grads.append(ds.astype(bf16))
            rows_h = slice(h * DH, (h + 1) * DH)
            dq_t[rows_h] += matmul(k_t[rows_h, at], grads[h])
        dv[at, :] += matmul(jnp.concatenate(probs, axis=1), do_lanes[...])
        dk[at, :] += matmul(jnp.concatenate(grads, axis=1), q_lanes[...])

    sweep(meta, first, block, step)
    out_ref[pl.ds(pl.multiple_of(first, block), block), 0:GP] = dq_t[...].T.astype(bf16)

    @pl.when(i == pl.num_programs(0) - 1)
    def _():
        def emit(t, carry):
            rows = pl.ds(pl.multiple_of(t * block, block), block)
            out_ref[rows, GP : 2 * GP] = dk[rows, :].astype(bf16)
            out_ref[rows, 2 * GP : 3 * GP] = dv[rows, :].astype(bf16)
            return carry

        lax.fori_loop(0, length // block, emit, 0)
        offset = lax.broadcasted_iota(jnp.int32, (block, block), 1) - lax.broadcasted_iota(
            jnp.int32, (block, block), 0
        )
        edges = [None] + thresholds()
        for h in range(GH):
            tails = []
            for at in edges:
                if at is None:
                    part = near[h, 0] + near[h, 1]
                else:
                    part = jnp.where(offset >= at, near[h, 0], 0.0) + jnp.where(
                        offset + block >= at, near[h, 1], 0.0
                    )
                tails.append(jnp.sum(part, axis=0, keepdims=True))
            for b in range(NB):
                if b + 1 < NB:
                    row = tails[b] - tails[b + 1]
                else:
                    row = tails[b] + far_sum[h : h + 1]
                tab_ref[h * NB + b : h * NB + b + 1] = row


def self_specs(parts, tok, length):
    block = tok // parts
    q_spec = pl.BlockSpec((block, GP), lambda i, m: (i * parts + sub_of(i, m[3], parts), 0))
    k_spec = pl.BlockSpec((length, GP), lambda i, m: (0, 1), pipeline_mode=pl.Buffered(1))
    v_spec = pl.BlockSpec((length, GP), lambda i, m: (0, 2), pipeline_mode=pl.Buffered(1))
    table_spec = pl.BlockSpec(memory_space=pltpu.SMEM)
    return table_spec, q_spec, k_spec, v_spec


def pair_count(length):
    return GH * length * length // 8


def self_forward(qkv, meta, table, parts, count, tok):
    length = qkv.shape[0]
    block = tok // parts
    rows = count * block
    return pl.pallas_call(
        functools.partial(self_forward_kernel, parts, tok),
        grid_spec=pltpu.PrefetchScalarGridSpec(
            num_scalar_prefetch=1,
            grid=(count,),
            in_specs=list(self_specs(parts, tok, length)),
            out_specs=[
                pl.BlockSpec((1, block, GL), lambda i, m: (i, 0, 0)),
                pl.BlockSpec((GL, block), lambda i, m: (0, i)),
                pl.BlockSpec((8, block), lambda i, m: (0, i)),
            ],
            scratch_shapes=[
                pltpu.VMEM((GP, length), bf16),
                pltpu.VMEM((GH, 2, block, block), f32),
                pltpu.VMEM((GP, block), f32),
                pltpu.VMEM((8, block), f32),
                pltpu.VMEM((8, block), f32),
                pltpu.VMEM((GH, GP, block), bf16),
            ],
        ),
        out_shape=[
            jax.ShapeDtypeStruct((count, block, GL), bf16),
            jax.ShapeDtypeStruct((GL, rows), f32),
            jax.ShapeDtypeStruct((8, rows), f32),
        ],
        compiler_params=pltpu.CompilerParams(vmem_limit_bytes=VMEM_LIMIT),
        cost_estimate=pl.CostEstimate(
            flops=pair_count(length) * 1024,
            transcendentals=pair_count(length),
            bytes_accessed=length * GP * 8,
        ),
        name="self_forward",
    )(meta, table, qkv, qkv, qkv)


def self_backward(qkv, meta, table, d_o, full, lse, parts, count, tok):
    length = qkv.shape[0]
    block = tok // parts
    return pl.pallas_call(
        functools.partial(self_backward_kernel, parts, tok),
        grid_spec=pltpu.PrefetchScalarGridSpec(
            num_scalar_prefetch=1,
            grid=(count,),
            in_specs=list(self_specs(parts, tok, length))
            + [
                pl.BlockSpec((1, block, GL), lambda i, m: (i, 0, 0)),
                pl.BlockSpec((GL, block), lambda i, m: (0, i)),
                pl.BlockSpec((8, block), lambda i, m: (0, i)),
            ],
            out_specs=[
                pl.BlockSpec((length, 3 * GP), lambda i, m: (0, 0), pipeline_mode=pl.Buffered(1)),
                pl.BlockSpec((GH * NB, block), lambda i, m: (0, 0)),
            ],
            scratch_shapes=[
                pltpu.VMEM((GP, length), bf16),
                pltpu.VMEM((GH, 2, block, block), f32),
                pltpu.VMEM((length, GP), f32),
                pltpu.VMEM((length, GP), f32),
                pltpu.VMEM((GP, block), f32),
                pltpu.VMEM((GH, 2, block, block), f32),
                pltpu.VMEM((8, block), f32),
                pltpu.VMEM((GH, GP, block), bf16),
                pltpu.VMEM((GH, GP, block), bf16),
                pltpu.VMEM((GH * block, GP), bf16),
                pltpu.VMEM((GH * block, GP), bf16),
                pltpu.VMEM((8, block), f32),
                pltpu.VMEM((block, GP), f32),
            ],
        ),
        out_shape=[
            jax.ShapeDtypeStruct((length, 3 * GP), bf16),
            jax.ShapeDtypeStruct((GH * NB, block), f32),
        ],
        compiler_params=pltpu.CompilerParams(vmem_limit_bytes=VMEM_LIMIT),
        cost_estimate=pl.CostEstimate(
            flops=pair_count(length) * 2560,
            transcendentals=pair_count(length),
            bytes_accessed=length * GP * 16,
        ),
        name="self_backward",
    )(meta, table, qkv, qkv, qkv, d_o, full, lse)


PAIR = 2 * DH


def pair_rows(x_t, h):
    zeros = jnp.zeros((DH, x_t.shape[1]), x_t.dtype)
    own = x_t[h * DH : (h + 1) * DH]
    return jnp.concatenate([own, zeros] if h == 0 else [zeros, own], axis=0)


def cross_forward_kernel(q_ref, k_ref, v_ref, o_ref, full_ref, lse_ref, v_t, q_t):
    tok = q_ref.shape[0]
    chunk = math.gcd(tok, 256)
    v_t[...] = flip(v_ref[...])
    q_t[...] = flip(q_ref[...])
    lse_ref[...] = jnp.zeros_like(lse_ref)
    for at in range(0, tok, chunk):
        cols = slice(at, at + chunk)
        for h in range(2):
            rows_h = slice(h * DH, (h + 1) * DH)
            s = matmul(k_ref[...], pair_rows(q_t[:, cols], h))
            top = fold(s, jnp.maximum)
            p = jnp.exp(s - top)
            total = fold(p, jnp.add)
            full_ref[rows_h, cols] = matmul(v_t[rows_h], p.astype(bf16)) / total
            lse_ref[h : h + 1, cols] = top + jnp.log(total)
    o_ref[...] = full_ref[...].T.astype(bf16)


def cross_backward_kernel(
    q_ref, k_ref, v_ref, do_ref, full_ref, lse_ref, dq_ref, dk_ref, dv_ref, k_t, q_t, do_t, dq_t,
    dk, dv,
):
    tok = q_ref.shape[0]
    chunk = math.gcd(tok, 256)
    k_t[...] = flip(k_ref[...])
    q_t[...] = flip(q_ref[...])
    do_t[...] = do_ref[...].astype(f32).T
    for at in range(0, tok, chunk):
        cols = slice(at, at + chunk)
        probs, grads, q_lanes, do_lanes = [], [], [], []
        for h in range(2):
            rows_h = slice(h * DH, (h + 1) * DH)
            s = matmul(k_ref[...], pair_rows(q_t[:, cols], h))
            p = jnp.exp(s - lse_ref[h : h + 1, cols])
            delta = jnp.sum(do_t[rows_h, cols] * full_ref[rows_h, cols], axis=0, keepdims=True)
            dp = matmul(v_ref[...], pair_rows(do_t[:, cols].astype(bf16), h))
            ds = (p * (dp - delta)).astype(bf16)
            probs.append(p.astype(bf16))
            grads.append(ds)
            dq_t[rows_h, cols] = matmul(k_t[rows_h], ds)
            q_lanes.append(head_lanes(q_ref[cols, :], h))
            do_lanes.append(head_lanes(do_ref[cols, :], h))
        part_v = matmul(jnp.concatenate(probs, axis=1), jnp.concatenate(do_lanes, axis=0))
        part_k = matmul(jnp.concatenate(grads, axis=1), jnp.concatenate(q_lanes, axis=0))
        if at == 0:
            dv[...] = part_v
            dk[...] = part_k
        else:
            dv[...] += part_v
            dk[...] += part_k
    dq_ref[...] = dq_t[...].T.astype(bf16)
    dk_ref[...] = dk[...].astype(bf16)
    dv_ref[...] = dv[...].astype(bf16)


def cross_forward(q, k, v):
    tok, enc = q.shape[0], k.shape[0]
    pairs = H // 2
    col = lambda p: (0, p)
    row = lambda p: (p, 0)
    return pl.pallas_call(
        cross_forward_kernel,
        grid=(pairs,),
        in_specs=[
            pl.BlockSpec((tok, PAIR), col),
            pl.BlockSpec((enc, PAIR), col),
            pl.BlockSpec((enc, PAIR), col),
        ],
        out_specs=[
            pl.BlockSpec((tok, PAIR), col),
            pl.BlockSpec((PAIR, tok), row),
            pl.BlockSpec((8, tok), row),
        ],
        out_shape=[
            jax.ShapeDtypeStruct((tok, D), bf16),
            jax.ShapeDtypeStruct((D, tok), f32),
            jax.ShapeDtypeStruct((8 * pairs, tok), f32),
        ],
        scratch_shapes=[pltpu.VMEM((PAIR, enc), bf16), pltpu.VMEM((PAIR, tok), bf16)],
        compiler_params=pltpu.CompilerParams(vmem_limit_bytes=VMEM_LIMIT),
        cost_estimate=pl.CostEstimate(
            flops=H * tok * enc * 1024, transcendentals=H * tok * enc, bytes_accessed=D * tok * 12
        ),
        name="cross_forward",
    )(q, k, v)


def cross_backward(q, k, v, d_o, full, lse):
    tok, enc = q.shape[0], k.shape[0]
    pairs = H // 2
    col = lambda p: (0, p)
    row = lambda p: (p, 0)
    return pl.pallas_call(
        cross_backward_kernel,
        grid=(pairs,),
        in_specs=[
            pl.BlockSpec((tok, PAIR), col),
            pl.BlockSpec((enc, PAIR), col),
            pl.BlockSpec((enc, PAIR), col),
            pl.BlockSpec((tok, PAIR), col),
            pl.BlockSpec((PAIR, tok), row),
            pl.BlockSpec((8, tok), row),
        ],
        out_specs=[
            pl.BlockSpec((tok, PAIR), col),
            pl.BlockSpec((enc, PAIR), col),
            pl.BlockSpec((enc, PAIR), col),
        ],
        out_shape=[
            jax.ShapeDtypeStruct((tok, D), bf16),
            jax.ShapeDtypeStruct((enc, D), bf16),
            jax.ShapeDtypeStruct((enc, D), bf16),
        ],
        scratch_shapes=[
            pltpu.VMEM((PAIR, enc), bf16),
            pltpu.VMEM((PAIR, tok), bf16),
            pltpu.VMEM((PAIR, tok), f32),
            pltpu.VMEM((PAIR, tok), f32),
            pltpu.VMEM((enc, PAIR), f32),
            pltpu.VMEM((enc, PAIR), f32),
        ],
        compiler_params=pltpu.CompilerParams(vmem_limit_bytes=VMEM_LIMIT),
        cost_estimate=pl.CostEstimate(
            flops=H * tok * enc * 2560, transcendentals=H * tok * enc, bytes_accessed=D * tok * 20
        ),
        name="cross_backward",
    )(q, k, v, d_o, full, lse)


LANES = 128


def gelu_pair(v):
    inner = math.sqrt(2 / math.pi) * (v + 0.044715 * (v * v * v))
    t = jnp.tanh(inner)
    half = 0.5 * (1.0 + t)
    slope = half + 0.5 * v * (1.0 - t * t) * (
        math.sqrt(2 / math.pi) * (1.0 + 3 * 0.044715 * (v * v))
    )
    return v * half, slope


def ffn_kernel(
    x_ref, c_ref, gate_ref, up_ref, down_ref, out_ref, gx_ref, dw_ref, x_t
):
    f = pl.program_id(0)

    @pl.when(f == 0)
    def _():
        x_t[...] = flip(x_ref[...])
        out_ref[...] = jnp.zeros_like(out_ref)
        gx_ref[...] = jnp.zeros_like(gx_ref)

    def emit(g, at):
        for lane in range(0, g.shape[1], LANES):
            dw_ref[0, 0, at : at + g.shape[0]] = g[:, lane : lane + LANES].astype(bf16)
            at += g.shape[0]
        return at

    x = x_ref[...]
    c = c_ref[...]
    w_gate, w_up, w_down = gate_ref[0], up_ref[0], down_ref[0]
    gate = matmul(x, w_gate)
    up = matmul(x, w_up)
    act, slope = gelu_pair(gate)
    hidden_full = act * up
    hidden = hidden_full.astype(bf16)
    out_ref[...] += matmul(hidden, w_down)
    grad_hidden = right_matmul(c, w_down)
    at = emit(matmul(flip(hidden), c), 0)
    grad_gate = (grad_hidden * up * slope).astype(bf16)
    grad_up = (grad_hidden * act).astype(bf16)
    at = emit(matmul(x_t[...], grad_gate), at)
    at = emit(matmul(x_t[...], grad_up), at)
    gx_ref[...] += right_matmul(grad_gate, w_gate) + right_matmul(grad_up, w_up)


def ffn(x, c, gate, up, down):
    tok = x.shape[0]
    parts, _, width = gate.shape
    whole = pl.BlockSpec((tok, D), lambda f: (0, 0))
    wide = pl.BlockSpec((1, D, width), lambda f: (f, 0, 0))
    tall = pl.BlockSpec((1, width, D), lambda f: (f, 0, 0))
    total = parts * width
    lines = 3 * D * width // LANES
    return pl.pallas_call(
        ffn_kernel,
        grid=(parts,),
        in_specs=[whole, whole, wide, wide, tall],
        out_specs=[
            whole,
            whole,
            pl.BlockSpec((1, 1, lines, LANES), lambda f: (f % 2, f // 2, 0, 0)),
        ],
        out_shape=[
            jax.ShapeDtypeStruct((tok, D), f32),
            jax.ShapeDtypeStruct((tok, D), f32),
            jax.ShapeDtypeStruct((2, parts // 2, lines, LANES), bf16),
        ],
        scratch_shapes=[pltpu.VMEM((D, tok), bf16)],
        compiler_params=pltpu.CompilerParams(vmem_limit_bytes=VMEM_LIMIT),
        cost_estimate=pl.CostEstimate(
            flops=18 * tok * D * total, transcendentals=tok * total, bytes_accessed=12 * D * total
        ),
        name="feed_forward",
    )(x, c, gate, up, down)


def split_ffn(flat, width):
    down = flat[: 6 * width].reshape(6, width, LANES)
    rest = flat[6 * width :].reshape(2, width // LANES, D, LANES)
    join = lambda x: jnp.concatenate([x[i] for i in range(x.shape[0])], axis=1)
    return join(rest[0]), join(rest[1]), join(down)


def weights_kernel(rows, *refs):
    out_ref = refs[-1]
    for i in range(len(refs) // 2):
        g = matmul(flip(refs[2 * i][...]), refs[2 * i + 1][...]).astype(bf16)
        for f in range(D // rows):
            out_ref[f % 2, f // 2, i * rows : (i + 1) * rows] = g[f * rows : (f + 1) * rows]


def weight_grads(pairs, rows):
    count = len(pairs)
    owners = D // rows
    flat = [x for pair in pairs for x in pair]
    return pl.pallas_call(
        functools.partial(weights_kernel, rows),
        out_shape=jax.ShapeDtypeStruct((2, owners // 2, count * rows, D), bf16),
        compiler_params=pltpu.CompilerParams(vmem_limit_bytes=VMEM_LIMIT),
        cost_estimate=pl.CostEstimate(
            flops=sum(2 * D * D * x.shape[0] for x, _ in pairs),
            transcendentals=0,
            bytes_accessed=sum(x.size * 2 for x in flat) + 2 * count * D * D,
        ),
        name="weight_grads",
    )(*flat)


def shards(
    inputs,
    encoded,
    doc_lengths,
    self_gain,
    self_query,
    self_key,
    self_value,
    self_output,
    bias_table,
    cross_gain,
    cross_query,
    cross_key,
    cross_value,
    cross_output,
    ffn_gain,
    ffn_gate,
    ffn_up,
    ffn_down,
    cotangent,
):
    count = lax.axis_size("ctx")
    owners = lax.axis_size("fsdp")
    parts = count // GROUPS
    lines = count // 2
    me = lax.axis_index("ctx")
    group, split = me // parts, me % parts
    line, side = me // 2, me % 2
    tok = inputs.shape[1]
    enc = encoded.shape[1]
    block = tok // parts
    half = owners // 2
    owner_me = lax.axis_index("fsdp")
    core = owner_me % 2
    length = count * tok
    rows = self_query.shape[0]

    swap = [(i, i ^ 1) for i in range(count)]
    ring = [(i, (i + 2) % count) for i in range(count)]

    def columns(w):
        return jnp.pad(
            lax.dynamic_slice(w, (0, group * GL), (rows, GL)), ((0, 0), (0, GP - GL))
        )

    def as_row(v):
        v = v.reshape(1, -1)
        return jnp.pad(v, ((0, 0), (0, 3 * GP - v.shape[1])))

    packed = jnp.concatenate(
        [columns(self_query), columns(self_key), columns(self_value)], axis=1
    )
    packed = jnp.concatenate(
        [packed, as_row(jnp.concatenate([self_gain, cross_gain, ffn_gain])), as_row(bias_table)],
        axis=0,
    )
    packed = jnp.pad(packed, ((0, 14), (0, 0)))
    packed = packed[None]
    while packed.shape[0] < owners:
        step = packed.shape[0]
        theirs = lax.ppermute(packed, "fsdp", [(i, i ^ step) for i in range(owners)])
        upper = (lax.axis_index("fsdp") // step) % 2 == 1
        packed = jnp.concatenate(
            [jnp.where(upper, theirs, packed), jnp.where(upper, packed, theirs)], axis=0
        )
    w_qkv = packed[:, :rows].reshape(D, 3 * GP)
    gains = packed[:, rows, : 3 * rows].reshape(owners, 3, rows).transpose(1, 0, 2).reshape(3, D)
    gains = gains.astype(f32)
    gain_self, gain_cross, gain_ffn = gains[0], gains[1], gains[2]
    table_all = packed[:, rows + 1, : bias_table.size].reshape(NB, H).astype(f32)
    table = lax.dynamic_slice(table_all, (0, group * GH), (NB, GH))
    sizes = doc_lengths[0]
    ends = [sizes[0], sizes[0] + sizes[1], sizes[0] + sizes[1] + sizes[2]]
    meta = jnp.stack(ends + [split]).astype(jnp.int32)

    def project(x):
        v = x.astype(f32)
        normed = (v * inverse_rms(v) * gain_self).astype(bf16)
        return normed, matmul(normed, w_qkv).astype(bf16)

    normed_all = jnp.zeros((length, D), bf16)
    qkv = jnp.zeros((length, 3 * GP), bf16)
    encoder = jnp.zeros((count * enc, D), bf16)
    piece = jnp.concatenate([inputs[0], encoded[0]], axis=0)
    def place(arrived, blocks):
        normed_all, qkv, encoder = blocks
        for x, owner in arrived:
            normed, projected = project(x[:tok])
            encoder = lax.dynamic_update_slice(encoder, x[tok:], (owner * enc, 0))
            normed_all = lax.dynamic_update_slice(normed_all, normed, (owner * tok, 0))
            qkv = lax.dynamic_update_slice(qkv, projected, (owner * tok, 0))
        return normed_all, qkv, encoder

    blocks = (normed_all, qkv, encoder)
    for s in range(lines):
        at = (line - s) % lines
        beside = lax.ppermute(piece, "ctx", swap)
        mine = piece
        if s + 1 < lines:
            piece = lax.ppermute(piece, "ctx", ring)
            mine, beside, piece = lax.optimization_barrier((mine, beside, piece))
        blocks = place([(mine, 2 * at + side), (beside, 2 * at + 1 - side)], blocks)
    normed_all, qkv, encoder = blocks

    qkv, normed_all, encoder = lax.optimization_barrier((qkv, normed_all, encoder))
    gather = lambda w: lax.all_gather(w, "fsdp", axis=0, tiled=True)
    w_output = gather(self_output)
    c_query = gather(cross_query)
    c_key = gather(cross_key)
    c_value = gather(cross_value)
    c_output = gather(cross_output)
    w_gate = lax.all_gather(ffn_gate, "fsdp", axis=0)
    w_up = lax.all_gather(ffn_up, "fsdp", axis=0)
    w_down = lax.all_gather(ffn_down, "fsdp", axis=0)

    out_chunks, self_full, lse = self_forward(qkv, meta, table, parts, count, tok)

    def turned(x):
        even = me % 2 == 0
        return jnp.stack(
            [jnp.where(even, x[:, s], x[:, parts - 1 - s]) for s in range(parts)], axis=1
        )

    def to_owner(chunks):
        got = lax.all_to_all(chunks, "ctx", 0, 0, tiled=True)
        got = got.reshape(GROUPS, parts, block, GL)
        return turned(got).transpose(1, 2, 0, 3).reshape(tok, D)

    def to_groups(x):
        got = x.reshape(GROUPS, parts, block, GL)
        got = turned(got)
        return lax.all_to_all(got.reshape(count, block, GL), "ctx", 0, 0, tiled=True)

    core_pairs = [(i, i ^ 1) for i in range(owners)]
    core_groups = [[b + 2 * i for i in range(half)] for b in range(2)]
    group_groups = [[g * parts + s for g in range(GROUPS)] for s in range(parts)]

    def add_up(x):
        return jnp.sum(x.astype(f32), axis=0)

    def pick(g, i, axis=0):
        return lax.dynamic_index_in_dim(g, i, axis, keepdims=False)

    def swap_cores(g, axis=0):
        got = lax.ppermute(pick(g, 1 - core, axis), "fsdp", core_pairs)
        return (pick(g, core, axis).astype(f32) + got.astype(f32)).astype(bf16)

    def over_chips(g):
        chip = owner_me // 2
        got = [pick(g, chip)]
        for k in range(1, half):
            route = [(i, (i // 2 + k) % half * 2 + i % 2) for i in range(owners)]
            got.append(lax.ppermute(pick(g, (chip + k) % half), "fsdp", route))
        return got

    def over_splits(g):
        got = [g]
        for k in range(1, parts):
            route = [(i, i // parts * parts + (i % parts + k) % parts) for i in range(count)]
            got.append(lax.ppermute(g, "ctx", route))
        return got

    def total(got):
        return sum(x.astype(f32) for x in got)

    def over_ctx(g):
        g = g.astype(bf16).reshape(count, g.shape[0] // count, g.shape[1])
        return lax.all_to_all(g, "ctx", 0, 0, tiled=True)

    def over_groups(g):
        g = jnp.broadcast_to(g[None], (GROUPS,) + g.shape)
        return lax.all_to_all(g, "ctx", 0, 0, tiled=True, axis_index_groups=group_groups)

    def whole(g):
        return lax.all_gather(g.astype(bf16), "ctx", axis=0, tiled=True).astype(f32)

    attended = to_owner(out_chunks)
    states = inputs[0].astype(f32)
    first_sum = states + matmul(attended, w_output)
    normed_two = (first_sum * inverse_rms(first_sum) * gain_cross).astype(bf16)
    cross_queries = matmul(normed_two, c_query).astype(bf16)
    cross_keys = matmul(encoder, c_key).astype(bf16)
    cross_values = matmul(encoder, c_value).astype(bf16)
    cross_out, cross_full, cross_lse = cross_forward(cross_queries, cross_keys, cross_values)
    second_sum = first_sum + matmul(cross_out, c_output)
    normed_three = (second_sum * inverse_rms(second_sum) * gain_ffn).astype(bf16)
    outer = cotangent[0]
    down_out, grad_three, d_ffn = ffn(normed_three, outer, w_gate, w_up, w_down)
    outputs = (second_sum + down_out).astype(bf16)
    d_ffn = swap_cores(d_ffn)

    grad_part, grad_gain_ffn = norm_back(second_sum, gain_ffn, grad_three)
    grad_second = outer.astype(f32) + grad_part
    branch_two = grad_second.astype(bf16)
    grad_cross_out = right_matmul(branch_two, c_output).astype(bf16)
    grad_cross_out, d_ffn = lax.optimization_barrier((grad_cross_out, d_ffn))
    grad_cq, grad_ck, grad_cv = cross_backward(
        cross_queries, cross_keys, cross_values, grad_cross_out, cross_full, cross_lse
    )
    d_ffn = over_chips(d_ffn)
    grad_part, grad_gain_cross = norm_back(first_sum, gain_cross, right_matmul(grad_cq, c_query))
    grad_first = grad_second + grad_part
    branch_one = grad_first.astype(bf16)
    grad_attended = jnp.einsum(
        "td,gcd->gtc", branch_one, w_output.reshape(GROUPS, GL, D), preferred_element_type=f32
    ).astype(bf16)
    d_o = to_groups(grad_attended)
    grad_enc = (right_matmul(grad_ck, c_key) + right_matmul(grad_cv, c_value)).astype(bf16)
    d_rest = swap_cores(
        weight_grads(
            [
                (attended, branch_one),
                (normed_two, grad_cq),
                (encoder, grad_ck),
                (encoder, grad_cv),
                (cross_out, branch_two),
            ],
            rows,
        )
    )
    grad_enc = lax.psum_scatter(grad_enc, "ctx", scatter_dimension=0, tiled=True)
    d_ffn = total(d_ffn).astype(bf16)
    d_o, d_ffn, d_rest = lax.optimization_barrier((d_o, d_ffn, d_rest))

    d_ffn = over_ctx(d_ffn)
    d_rest = over_chips(d_rest)
    d_qkv, table_rows = self_backward(qkv, meta, table, d_o, self_full, lse, parts, count, tok)
    d_qkv, d_ffn, d_rest, grad_enc = lax.optimization_barrier((d_qkv, d_ffn, d_rest, grad_enc))

    def partial_at(at):
        return right_matmul(lax.dynamic_slice(d_qkv, (at * tok, 0), (tok, 3 * GP)), w_qkv)

    travelling = None
    for s in range(1, lines + 1):
        at = (line - s) % lines
        leaving = partial_at(2 * at + 1 - side).astype(bf16)
        if s == 1:
            leaving, d_qkv, d_ffn, d_rest = lax.optimization_barrier(
                (leaving, d_qkv, d_ffn, d_rest)
            )
        theirs = lax.ppermute(leaving, "ctx", swap)
        both = partial_at(2 * at + side) + theirs.astype(f32)
        if travelling is not None:
            both = both + lax.ppermute(travelling.astype(bf16), "ctx", ring).astype(f32)
        travelling = both
    grad_one = travelling

    d_gate, d_up, d_down = split_ffn(whole(add_up(d_ffn)), ffn_gate.shape[1])
    d_rest = whole(add_up(over_ctx(total(d_rest))))
    d_rest = [d_rest[i * rows : (i + 1) * rows] for i in range(5)]
    d_output, d_c_query, d_c_key, d_c_value, d_c_output = d_rest

    d_w = left_matmul(normed_all, d_qkv).astype(bf16).reshape(owners, rows, 3 * GP)
    wide = lambda x: jnp.pad(x, ((0, 0), (0, 3 * GP - x.shape[1])))
    table_part = jnp.sum(table_rows, axis=1)[None]
    gain_part = jnp.stack([grad_gain_cross, grad_gain_ffn]).reshape(2, owners, rows)
    extra = jnp.stack(
        [
            jnp.broadcast_to(wide(table_part), (owners, 3 * GP)),
            wide(gain_part[0]),
            wide(gain_part[1]),
        ],
        axis=1,
    )
    extra = jnp.pad(extra, ((0, 0), (0, 13), (0, 0))).astype(bf16)
    d_w = jnp.concatenate([d_w, extra], axis=1)
    d_w = swap_cores(d_w.reshape((half, 2) + d_w.shape[1:]), 1)
    d_w = total(over_chips(d_w)).astype(bf16)
    d_w = total(over_splits(d_w)).astype(bf16)
    d_w = over_groups(d_w).astype(f32)
    grad_table = d_w[:, rows, : GH * NB].reshape(H, NB).T
    grad_gain_cross = jnp.sum(d_w[:, rows + 1, :rows], axis=0)
    grad_gain_ffn = jnp.sum(d_w[:, rows + 2, :rows], axis=0)
    d_w = [
        jnp.concatenate([d_w[g, :rows, i * GP : i * GP + GL] for g in range(GROUPS)], axis=1)
        for i in range(3)
    ]
    grad_gain_self = sum(
        jnp.sum(w.astype(f32) * d, axis=1)
        for w, d in zip((self_query, self_key, self_value), d_w)
    ) / self_gain.astype(f32)

    grad_part, _ = norm_back(states, gain_self, grad_one)
    grad_states = (grad_first + grad_part).astype(bf16)
    own_table = lax.dynamic_slice(
        grad_table, (owner_me * (NB // owners), 0), (NB // owners, H)
    )
    return (
        outputs[None],
        grad_states[None],
        grad_enc[None],
        grad_gain_self,
        d_w[0],
        d_w[1],
        d_w[2],
        d_output,
        own_table,
        grad_gain_cross,
        d_c_query,
        d_c_key,
        d_c_value,
        d_c_output,
        grad_gain_ffn,
        d_gate,
        d_up,
        d_down,
    )


def solution(mesh):
    tokens = P("fsdp", "ctx", None)
    row = P("fsdp", None)
    col = P(None, "fsdp")
    vec = P("fsdp")
    in_specs = (
        (tokens, tokens, row, vec, row, row, row, row, row, vec, row, row, row, row, vec)
        + (col, col, row, tokens)
    )
    out_specs = (
        (tokens, tokens, tokens, vec, row, row, row, row, row, vec, row, row, row, row, vec)
        + (col, col, row)
    )
    return jax.shard_map(shards, mesh=mesh, in_specs=in_specs, out_specs=out_specs, check_vma=False)
```
